32 devices in a mesh: walk: 8 (over z, x), vec: 4 (over y, core).
Axes of the slice: x: 2, y: 2, z: 4, core: 2. Of those that a mesh axis runs over, the one named last changes fastest.
Arguments:
- walkers: bfloat16 [16, 2432, 768], P('walk')
- chol: bfloat16 [4, 8, 384, 4096], P('vec', 'walk'), may hold values from -6 to 6
- owners: int32 [4, 2], P('vec'), may hold values from 0 to 7
- branch_src: int32 [16], P('walk'), may hold values from 0 to 15, as said below
Outputs:
- branched: bfloat16 [16, 2432, 768], P('walk')
- force_bias: float32 [16, 8, 2], P('walk', 'vec')
- exchange: float32 [16, 2], P('walk')
The draws below stay inside these ranges and needn't reach their ends.
Inputs may be any that keep to these rules, and one draw needn't show every extreme that they name: `branch_src`: slot s takes its walker from the 2 walkers of block s // 2, or of the block before or after it (blocks taken cyclically).
All inputs are finite; a program needn't handle non-finite values.
Results may differ from the reference program's by a relative error of at most 0.0052.
Values may be sent and summed in bfloat16 or wider, within the bound.
A program may use at most 192 MiB of HBM per device.

```python
import jax
import jax.numpy as jnp
from jax import lax

NORB = 2048
NE = 384
W_DEV = 2
G_USE = 2
WALKERS = 16
N_WALK = 8
N_VEC = 4


def draw_walkers(key, part):
    first, second = jax.random.split(key)
    orbital = jax.random.normal(first, (WALKERS, NORB, 2 * NE), jnp.float32)
    inverse = jax.random.normal(second, (WALKERS, NE, 2 * NE), jnp.float32)
    orbital = orbital * NORB ** (-0.5)
    inverse = inverse * (0.5 / NE)
    return jnp.concatenate([orbital, inverse], axis=1).astype(jnp.bfloat16)


def draw_branch_src(key, part):
    first, second = jax.random.split(key)
    slots = jnp.arange(WALKERS, dtype=jnp.int32)
    blocks = slots // W_DEV
    offset = jax.random.randint(first, (WALKERS,), -1, 2, dtype=jnp.int32)
    within = jax.random.randint(second, (WALKERS,), 0, W_DEV, dtype=jnp.int32)
    count = WALKERS // W_DEV
    return ((blocks + offset + count) % count * W_DEV + within).astype(jnp.int32)


def set_ends(values, own_key, low, high):
    index_at = [jax.random.randint(jax.random.fold_in(own_key, axis), (), 0, length) for axis, length in enumerate(values.shape)]
    widest = values.shape.index(max(values.shape))
    beside = index_at[:widest] + [(index_at[widest] + 1) % values.shape[widest]] + index_at[widest + 1:]
    return values.at[tuple(index_at)].set(low).at[tuple(beside)].set(high)


def steps_of(rng, shape, cuts, least, high):
    gain, own = 1.0, jax.random.fold_in(rng, 6)
    for position, blocks in cuts:
        draws = jnp.exp(jax.random.uniform(jax.random.fold_in(own, position), (blocks,), jnp.float32, least / len(cuts), high / len(cuts)))
        gain = gain * jnp.repeat(draws, shape[position] // blocks).reshape([-1 if axis == position else 1 for axis in range(len(shape))])
    return gain


def normal_values(stream_key, dims, scale, bound, shards=(), held_as=jnp.bfloat16):
    entries = jax.random.normal(stream_key, dims, jnp.float32) * scale
    if len(shards) > 0:
        entries = steps_of(stream_key, dims, shards, -0.22, 0.18) * entries
    return jnp.clip(entries, min=-bound, max=bound).astype(held_as)


def setup_inputs(seed: int = 0) -> dict:
    arg_keys = jax.random.split(jax.random.key(seed), 5)
    return {
        "walkers": draw_walkers(jax.random.fold_in(arg_keys[4], 71), 0),
        "chol": normal_values(arg_keys[1], (N_VEC, N_WALK, NE, 2 * NORB), 1.0, 6.0, ((0, 4), (1, 8))),
        "owners": set_ends(jax.random.randint(arg_keys[2], (N_VEC, G_USE), 0, N_WALK), jax.random.fold_in(arg_keys[2], 1), 0, N_WALK - 1).astype(jnp.int32),
        "branch_src": draw_branch_src(jax.random.fold_in(arg_keys[4], 71), 0),
    }


def complex_block(part):
    half = part.shape[1] // 2
    lower = jnp.concatenate([-part[:, half:], part[:, :half]], axis=1)
    return jnp.concatenate([part, lower], axis=0)


def reference(walkers, chol, owners, branch_src):
    branched = walkers[branch_src]
    picked = chol[jnp.arange(N_VEC)[:, None], owners]
    stacked = picked.reshape(N_VEC * G_USE * NE, 2 * NORB)

    def per_walker(state):
        pbig = complex_block(state[:NORB])
        obig = complex_block(state[NORB:]).astype(jnp.float32)
        mixed = jnp.dot(stacked, pbig, preferred_element_type=jnp.float32).astype(jnp.bfloat16)
        mixed = mixed.reshape(N_VEC * G_USE, NE, 2 * NE).astype(jnp.float32)
        green = jnp.einsum('gik,kj->gij', mixed, obig, precision=lax.Precision.HIGHEST)
        real = green[:, :, :NE]
        imag = green[:, :, NE:]
        bias = jnp.stack([jnp.trace(real, axis1=1, axis2=2), jnp.trace(imag, axis1=1, axis2=2)], axis=1)
        real_t = jnp.swapaxes(real, 1, 2)
        imag_t = jnp.swapaxes(imag, 1, 2)
        ex_real = jnp.sum(real * real_t - imag * imag_t)
        ex_imag = 2.0 * jnp.sum(real * imag_t)
        return bias, -0.5 * jnp.stack([ex_real, ex_imag])

    force_bias, exchange = lax.map(per_walker, branched)
    return branched, force_bias, exchange
```

```python
import functools

import jax
import jax.numpy as jnp
from jax import lax
from jax.experimental import pallas as pl
from jax.experimental.pallas import tpu as pltpu
from jax.sharding import PartitionSpec as P

MESH = pl.DeviceIdType.MESH
LANES = 128
DEEP = 4
UNIT = 32
GROUP = 2
SKEW = 2
AHEAD = 3
X_SLOW = (16, 100)
X_FAST = 2
X_HUB = (16, 17, 18, 19, 20, 21, 23, 24, 25, 25)
X_LEAF = (3, 5, 7, 8, 10, 11, 12, 14, 15, 16)
Y_LAG = 3
LOAD_LAG = 2
CATCH_UP = 1
Z_HUB = (16, 3, 4)
Z_LEAF = (3, 5, 9)
Z_LAG = 3
Z_LAG_Y = 3
NEAR = 38
SPAN = 8


def flip(index):
    return index + 1 - 2 * lax.rem(index, 2)


def clip(value, low, high):
    return jnp.minimum(jnp.maximum(value, low), high)


def step_kernel(
    n_walk, n_vec, flags, chol, walkers, table, partner, beyond,
    home, away, up, down, mat, state, acc, result,
    home_sem, away_sem, up_sem, down_sem,
    mate_send, across_send, relay_send, up_send, down_send,
    x_send, y_send, d_send, r_send, z_send, zy_send, zd_send, zr_send,
    x_sem, y_sem, d_sem, r_sem, z_sem, zy_sem, zd_sem, zr_sem,
    load_sem, t_send, t_sem,
):
    walk, vec = lax.axis_index("walk"), lax.axis_index("vec")
    rows = n_walk // 2
    last = rows - 1
    row, col = walk // 2, lax.rem(walk, 2)
    low = lax.rem(vec, 2)
    hub = low == col
    leaf = jnp.logical_not(hub)
    pieces, electrons = home.shape[0], home.shape[1]
    blocks = pieces // DEEP
    per_dev = walkers.shape[0]
    quarter = walkers.shape[1] // n_vec
    units = quarter // UNIT
    groups = [(first, min(GROUP, units - first)) for first in range(0, units, GROUP)]
    ends = [first + size for first, size in groups]
    flip_walk, flip_vec = flip(walk), flip(vec)
    far_vec = lax.rem(vec + 2, n_vec)
    z_next = lax.rem(row + 1 - 2 * col + rows, rows)
    z_to = {"walk": z_next * 2 + col, "vec": vec}
    across = {"walk": flip_walk, "vec": vec}
    mate = {"walk": walk, "vec": flip_vec}
    over = {"walk": walk, "vec": far_vec}
    above = {"walk": walk + 2, "vec": vec}
    below = {"walk": walk - 2, "vec": vec}
    row_up, row_down = lax.rem(row + 1, rows), lax.rem(row + rows - 1, rows)

    place = col * n_vec + vec
    readers = [({"walk": walk, "vec": lax.rem(vec + j, n_vec)}, place) for j in range(1, n_vec)]
    readers += [({"walk": flip_walk, "vec": lax.rem(vec + j, n_vec)}, place) for j in range(n_vec)]
    readers += [({"walk": row_up * 2, "vec": lax.rem(vec + j, n_vec)}, place + 2 * n_vec) for j in range(n_vec)]
    readers += [({"walk": row_down * 2 + 1, "vec": lax.rem(vec + j, n_vec)}, place + 2 * n_vec) for j in range(n_vec)]

    def each(lo, hi, f):
        def body(k, carry):
            f(k)
            return carry
        lax.fori_loop(lo, hi, body, 0)

    def remote(src, dst, send, recv, target):
        return pltpu.make_async_remote_copy(
            src_ref=src, dst_ref=dst, send_sem=send, recv_sem=recv,
            device_id=target, device_id_type=MESH)

    def chol_piece(k):
        b, j = lax.div(k, DEEP), lax.rem(k, DEEP)
        half = DEEP // 2
        at = b * half + jnp.where(j < half, j, j - half + blocks * half)
        return chol.at[0, 0, :, pl.ds(pl.multiple_of(at * LANES, LANES), LANES)]

    def own_to_home(k):
        return pltpu.make_async_copy(chol_piece(k), home.at[k], home_sem.at[k])

    def own_to_mate(k):
        return remote(chol_piece(k), home.at[k], mate_send, home_sem.at[k], mate)

    def own_across(k):
        return remote(chol_piece(k), away.at[k], across_send, away_sem.at[k], across)

    def away_to_mate(k):
        return remote(away.at[k], away.at[k], relay_send, away_sem.at[k], mate)

    def send_up(k):
        return remote(up.at[k], up.at[k], up_send, up_sem.at[k], above)

    def send_down(k):
        return remote(down.at[k], down.at[k], down_send, down_sem.at[k], below)

    def unit_rows(u):
        return pl.ds(pl.multiple_of(vec * quarter + u * UNIT, UNIT), UNIT)

    def x_unit(u):
        at = unit_rows(u)
        return remote(walkers.at[:, at], partner.at[:, at], x_send, x_sem.at[lax.div(u, GROUP)], across)

    def z_unit(u):
        at = unit_rows(u)
        return remote(partner.at[:, at], beyond.at[:, at], z_send, z_sem.at[lax.div(u, GROUP)], z_to)

    def group(buffer, n, index, send, recv, target):
        first, size = groups[n]
        at = pl.ds(pl.multiple_of(index * quarter + first * UNIT, UNIT), size * UNIT)
        return remote(buffer.at[:, at], buffer.at[:, at], send, recv.at[n], target)

    def load(w):
        src = walkers.at[w] if w < per_dev else partner.at[w - per_dev]
        return pltpu.make_async_copy(src, state.at[w], load_sem.at[w])

    for w in range(per_dev):
        load(w).start()

    @pl.when(hub)
    def _():
        each(0, pieces, lambda k: own_to_home(k).start())

    bar = pltpu.get_barrier_semaphore()
    for target in (
        [t for t, _ in readers[:2 * n_vec - 1]]
        + [{"walk": r * 2 + c, "vec": lax.rem(vec + j, n_vec)}
           for r in (row_up, row_down) for c in range(2) for j in range(n_vec)]
    ):
        pl.semaphore_signal(bar, inc=1, device_id=target, device_id_type=MESH)
    pl.semaphore_wait(bar, 6 * n_vec - 1)

    @pl.when(hub)
    def _():
        each(0, min(AHEAD, pieces), lambda k: own_to_mate(k).start())
        each(0, units, lambda u: x_unit(u).start())

    @pl.when(leaf)
    def _():
        def x_count(k):
            slow = lax.div(jnp.minimum(k, X_SLOW[0]), X_SLOW[1])
            return jnp.minimum(slow + jnp.maximum(k - X_SLOW[0], 0) * X_FAST, units)

        def start(k):
            own_across(k).start()
            each(x_count(k), x_count(k + 1), lambda u: x_unit(u).start())
        each(0, pieces, start)
        each(x_count(pieces), units, lambda u: x_unit(u).start())

    acc[...] = jnp.zeros_like(acc)

    here = flags[0] == 1
    below_or_here = flags[1] == 1
    from_home = flags[2] == 1
    total = pieces + SKEW * last
    depth = jnp.maximum(row, last - row)

    def sent(i):
        begin, gain, per = (jnp.where(hub, a, b) for a, b in zip(Z_HUB, Z_LEAF))
        return jnp.minimum(lax.div(jnp.maximum(i - begin, 0) * gain, per), units)

    def chain(i):
        @pl.when(i < pieces)
        def _():
            @pl.when(hub)
            def _():
                own_across(i).wait_recv()
                away_to_mate(i).start()

                @pl.when(i + AHEAD < pieces)
                def _():
                    own_to_mate(i + AHEAD).start()

                own_to_home(i).wait()

            @pl.when(leaf)
            def _():
                own_to_mate(i).wait_recv()
                away_to_mate(i).wait_recv()

        ku = i - SKEW * row
        kd = i - SKEW * (last - row)

        @pl.when(jnp.logical_and(ku >= 0, ku < pieces))
        def _():
            own = jnp.where(from_home, home[ku], away[ku])

            @pl.when(row == 0)
            def _():
                up[ku] = own

            @pl.when(row > 0)
            def _():
                send_up(ku).wait_recv()
                up[ku] = jnp.where(here, own, up[ku])

            @pl.when(row < last)
            def _():
                send_up(ku).start()

        @pl.when(jnp.logical_and(kd >= 0, kd < pieces))
        def _():
            own = jnp.where(from_home, home[kd], away[kd])

            @pl.when(row == last)
            def _():
                down[kd] = own

            @pl.when(row < last)
            def _():
                send_down(kd).wait_recv()
                down[kd] = jnp.where(here, own, down[kd])

            @pl.when(row > 0)
            def _():
                send_down(kd).start()

        done = i - SKEW * depth

        @pl.when(jnp.logical_and(done >= 0, done < pieces))
        def _():
            mat[done] = jnp.where(below_or_here, up[done], down[done])

    load_at = X_HUB[-1] + Y_LAG + LOAD_LAG

    def arrive(n):
        group(partner, n, vec, x_send, x_sem, across).wait_recv()
        group(partner, n, vec, y_send, y_sem, over).start()
        group(partner, n, vec, d_send, d_sem, mate).start()

    def pass_on(n):
        group(partner, n, far_vec, y_send, y_sem, over).wait_recv()
        group(partner, n, far_vec, r_send, r_sem, mate).start()

    def load_partner():
        for n in range(len(groups)):
            group(partner, n, vec, d_send, d_sem, mate).wait_recv()
            group(partner, n, vec, r_send, r_sem, mate).wait_recv()
        for w in range(per_dev):
            load(per_dev + w).start()

    def loaded(first):
        for w in range(per_dev):
            load(first + w).wait()

    def z_arrive(n):
        group(beyond, n, vec, z_send, z_sem, z_to).wait_recv()
        group(beyond, n, vec, zy_send, zy_sem, over).start()
        group(beyond, n, vec, zd_send, zd_sem, mate).start()

    def z_pass_on(n):
        group(beyond, n, far_vec, zy_send, zy_sem, over).wait_recv()
        group(beyond, n, far_vec, zr_send, zr_sem, mate).start()

    half = DEEP // 2
    wide = half * LANES

    def multiply(b, w):
        p = state[w, pl.ds(pl.multiple_of(b * wide, wide), wide), :]
        re = jnp.concatenate([mat[b * DEEP + j] for j in range(half)], axis=1)
        im = jnp.concatenate([mat[b * DEEP + half + j] for j in range(half)], axis=1)
        x = jnp.dot(re, p, preferred_element_type=jnp.float32)
        y = jnp.dot(im, p, preferred_element_type=jnp.float32)
        acc[w, :, :electrons] += x[:, :electrons] - y[:, electrons:]
        acc[w, :, electrons:] += x[:, electrons:] + y[:, :electrons]

    def products(i):
        e = i - SKEW * depth - (DEEP - 1)
        def own_count(e, w):
            return clip(lax.div(e + DEEP - w, DEEP), 0, blocks)

        def partner_count(i, w):
            e = i - SKEW * depth - (DEEP - 1)
            full = clip(lax.div(e + DEEP, DEEP), 0, blocks)
            return jnp.where(i > total, blocks, clip((i - load_at - 2) * CATCH_UP, 0, full))

        spans = [(own_count(e - 1, w), own_count(e, w)) for w in range(per_dev)]
        spans += [(partner_count(i - 1, w), partner_count(i, w)) for w in range(per_dev)]
        def some(w, carry):
            lo, hi = spans[-1]
            for v in range(len(spans) - 1):
                lo = jnp.where(w == v, spans[v][0], lo)
                hi = jnp.where(w == v, spans[v][1], hi)
            lax.fori_loop(lo, hi, lambda b, c: (multiply(b, w), c)[1], 0)
            return carry
        lax.fori_loop(0, len(spans), some, 0)

    sub = lax.broadcasted_iota(jnp.int32, result.shape, 0)
    lane = lax.broadcasted_iota(jnp.int32, result.shape, 1)
    result[...] = jnp.zeros_like(result)
    orbitals = blocks * wide

    def finish(w):
        o = state[w, orbitals:, :]
        m = acc[w].astype(jnp.bfloat16)
        u = jnp.dot(m[:, :electrons], o, preferred_element_type=jnp.float32)
        v = jnp.dot(m[:, electrons:], o, preferred_element_type=jnp.float32)
        g_re = u[:, :electrons] - v[:, electrons:]
        g_im = u[:, electrons:] + v[:, :electrons]
        t_re, t_im = g_re.T, g_im.T
        eye = (lax.broadcasted_iota(jnp.int32, g_re.shape, 0)
               == lax.broadcasted_iota(jnp.int32, g_re.shape, 1))
        values = [
            jnp.sum(jnp.where(eye, g_re, 0.0)),
            jnp.sum(jnp.where(eye, g_im, 0.0)),
            jnp.sum(g_re * t_re - g_im * t_im),
            2.0 * jnp.sum(g_re * t_im),
        ]
        for n, value in enumerate(values):
            result[...] = jnp.where(jnp.logical_and(sub == w, lane == n), value, result[...])

    def tell(n):
        target, where = readers[n]
        return remote(result, table.at[where], t_send.at[n], t_sem.at[where], target)

    def tell_all():
        for n in range(len(readers)):
            tell(n).start()

    events, rest = [], []
    for times, z_times, role in ((X_HUB, Z_HUB, hub), (X_LEAF, Z_LEAF, leaf)):
        late = []
        for n, end in enumerate(ends):
            at = times[min(n, len(times) - 1)]
            events.append((at, role, functools.partial(arrive, n)))
            events.append((at + Y_LAG, role, functools.partial(pass_on, n)))
            at = z_times[0] + -(-end * z_times[2] // z_times[1]) + Z_LAG
            for run, when in ((z_arrive, at), (z_pass_on, at + Z_LAG_Y)):
                if when < min(total, NEAR):
                    events.append((when, role, functools.partial(run, n)))
                else:
                    late.append((run, n))
        late.sort(key=lambda item: item[1] + (1 if item[0] is z_pass_on else 0))
        rest.append((role, late))
    events.append((load_at, None, functools.partial(load_partner)))
    events.append((load_at + 2, None, functools.partial(loaded, per_dev)))
    events.append((min(DEEP - 1 + SKEW * (rows // 2), total), None, functools.partial(loaded, 0)))

    def handle(start, stop):
        for role, late in rest:
            @pl.when(role)
            def _():
                for run, n in late[start:stop]:
                    run(n)

    after = [
        lambda: each(sent(total - 1), units, lambda u: z_unit(u).start()),
        functools.partial(handle, 0, 1),
        lambda: each(total, total + 2, products),
    ]
    for w in range(2 * per_dev):
        after.append(functools.partial(handle, w + 1, w + 2))
        after.append(functools.partial(finish, w))
    after.append(tell_all)
    after.append(functools.partial(handle, 2 * per_dev + 1, 10 * len(groups)))

    families = {}
    for when, role, run in events:
        families.setdefault((run.func, when // SPAN) if role is not None else None, []).append((when, role, run))

    def step(i):
        chain(i)
        each(sent(i - 1), sent(i), lambda u: z_unit(u).start())
        for members in families.values():
            times = [when for when, _, _ in members]

            @pl.when(jnp.logical_and(i >= min(times), i <= max(times)))
            def _():
                for when, role, run in members:
                    pl.when(i == when if role is None else jnp.logical_and(i == when, role))(run)
        products(i)

    each(0, total, step)
    for run in after:
        run()

    table[place] = result[...]

    for n in range(len(groups)):
        group(beyond, n, vec, zd_send, zd_sem, mate).wait_recv()
        group(beyond, n, vec, zr_send, zr_sem, mate).wait_recv()

    def all_sent(buffer, send, target):
        remote(buffer, buffer, send, t_sem.at[0], target).wait_send()

    @pl.when(hub)
    def _():
        all_sent(home, mate_send, mate)
        all_sent(away, relay_send, mate)

    @pl.when(leaf)
    def _():
        all_sent(away, across_send, across)

    @pl.when(row < last)
    def _():
        all_sent(up, up_send, above)

    @pl.when(row > 0)
    def _():
        all_sent(down, down_send, below)

    part = partner.at[:, pl.ds(pl.multiple_of(vec * quarter, UNIT), quarter)]
    for send, target in (
        (x_send, across), (y_send, over), (d_send, mate), (r_send, mate),
        (z_send, z_to), (zy_send, over), (zd_send, mate), (zr_send, mate),
    ):
        all_sent(part, send, target)

    for n in range(len(readers)):
        tell(n).wait_send()

    for j in range(1, n_vec):
        v = lax.rem(vec + j, n_vec)
        remote(result, table.at[0], t_send.at[0], t_sem.at[col * n_vec + v], mate).wait_recv()
    for j in range(n_vec):
        remote(result, table.at[0], t_send.at[0], t_sem.at[(1 - col) * n_vec + j], mate).wait_recv()
    for j in range(2 * n_vec):
        remote(result, table.at[0], t_send.at[0], t_sem.at[2 * n_vec + j], mate).wait_recv()


def step_all(n_walk, n_vec, flags, chol, walkers):
    per_dev, height, width = walkers.shape
    electrons, orbitals = chol.shape[2:]
    pieces = orbitals // LANES
    groups = -(-(height // n_vec // UNIT) // GROUP)
    big = pltpu.VMEM((pieces, electrons, LANES), chol.dtype)
    dma = pltpu.SemaphoreType.DMA
    any_spec = pl.BlockSpec(memory_space=pl.ANY)
    smem = pl.BlockSpec(memory_space=pltpu.SMEM)
    same = jax.ShapeDtypeStruct(walkers.shape, walkers.dtype)
    return pl.pallas_call(
        functools.partial(step_kernel, n_walk, n_vec),
        out_shape=(jax.ShapeDtypeStruct((4 * n_vec, 8, 128), jnp.float32), same, same),
        in_specs=[smem, any_spec, any_spec],
        out_specs=(pl.BlockSpec(memory_space=pltpu.VMEM), any_spec, any_spec),
        scratch_shapes=[
            big, big, big, big, big,
            pltpu.VMEM((2 * per_dev, height, width), walkers.dtype),
            pltpu.VMEM((2 * per_dev, electrons, width), jnp.float32),
            pltpu.VMEM((8, 128), jnp.float32),
        ] + [dma((pieces,))] * 4 + [dma] * 13 + [dma((groups,))] * 8
        + [dma((2 * per_dev,)), dma((4 * n_vec - 1,)), dma((4 * n_vec,))],
        compiler_params=pltpu.CompilerParams(
            collective_id=0, has_side_effects=True, vmem_limit_bytes=62 * 1024 * 1024),
        name="step_all",
    )(flags, chol, walkers)


BITS = 4


def branch_kernel(sources, walkers, partner, beyond, branched, held, in_sem, out_sem):
    per_dev, height = walkers.shape[:2]
    piece = height // BITS

    def rows(t):
        return pl.ds(t * piece, piece)

    def fetch(buffer, s, t):
        return pltpu.make_async_copy(
            buffer.at[lax.rem(sources[s], per_dev), rows(t)], held.at[s, rows(t)], in_sem.at[s, t])

    def put(s, t):
        return pltpu.make_async_copy(held.at[s, rows(t)], branched.at[s, rows(t)], out_sem.at[s, t])

    cases = [(s, t) for s in range(per_dev) for t in range(BITS)]
    for s in range(per_dev):
        for which, buffer in enumerate((walkers, partner, beyond)):
            @pl.when(lax.div(sources[s], per_dev) == which)
            def _():
                for t in range(BITS):
                    fetch(buffer, s, t).start()
    for s, t in cases:
        fetch(walkers, s, t).wait()
        put(s, t).start()
    for s, t in cases:
        put(s, t).wait()


def branch(sources, walkers, partner, beyond):
    per_dev = walkers.shape[0]
    dma = pltpu.SemaphoreType.DMA
    any_spec = pl.BlockSpec(memory_space=pl.ANY)
    return pl.pallas_call(
        branch_kernel,
        out_shape=jax.ShapeDtypeStruct(walkers.shape, walkers.dtype),
        in_specs=[pl.BlockSpec(memory_space=pltpu.SMEM), any_spec, any_spec, any_spec],
        out_specs=any_spec,
        scratch_shapes=[pltpu.VMEM(walkers.shape, walkers.dtype), dma((per_dev, BITS)), dma((per_dev, BITS))],
        compiler_params=pltpu.CompilerParams(vmem_limit_bytes=62 * 1024 * 1024),
        name="branch",
    )(sources, walkers, partner, beyond)


def shards(n_walk, n_vec, walkers, chol, owners, branch_src):
    per_dev = walkers.shape[0]
    walk, vec = lax.axis_index("walk"), lax.axis_index("vec")
    row, col, low = walk // 2, walk % 2, vec % 2
    swap = [(i, i + 1 - 2 * (i % 2)) for i in range(n_vec)]
    mate_roots = lax.ppermute(owners[0], "vec", swap)
    roots = jnp.where(low == col, owners[0], mate_roots)
    root = jnp.take(roots, low)
    flags = jnp.stack([root // 2 == row, root // 2 <= row, root % 2 == col]).astype(jnp.int32)
    total = per_dev * n_walk
    relative = ((branch_src - (walk - 1) * per_dev + total) % total).astype(jnp.int32)
    table, partner, beyond = step_all(n_walk, n_vec, flags, chol, walkers)
    table = table[:, :2 * per_dev, :4].reshape(2, 2, n_vec // 2, 2, 2, per_dev, 4)
    even, odd = table[:, 0], table[:, 1]
    first = jnp.stack([even[:, :, :, 0], odd[:, :, :, 1]], axis=2)
    second = jnp.stack([even[:, :, :, 1], odd[:, :, :, 0]], axis=2)
    both = jnp.stack([first, second], axis=1)
    both = jnp.transpose(both, (0, 1, 5, 2, 3, 4, 6)).reshape(4 * per_dev, n_vec, 2, 4)
    side = relative // per_dev
    block = jnp.where(side == 1, col, jnp.where(side == 2 * (1 - col), 1 - col, 3 - col))
    chosen = jnp.take(both, block * per_dev + relative % per_dev, axis=0)
    kind = jnp.where(side == 1, 0, jnp.where(side == 2 * (1 - col), 1, 2))
    branched = branch(kind * per_dev + relative % per_dev, walkers, partner, beyond)
    bias = lax.dynamic_slice_in_dim(chosen, vec, 1, axis=1)[:, 0, :, :2]
    energy = -0.5 * jnp.sum(chosen[..., 2:], axis=(1, 2))
    return (branched, bias, energy)


def solution(mesh):
    n_walk, n_vec = mesh.shape["walk"], mesh.shape["vec"]
    return jax.shard_map(
        functools.partial(shards, n_walk, n_vec),
        mesh=mesh,
        in_specs=(P("walk", None, None), P("vec", "walk", None, None), P("vec", None), P("walk")),
        out_specs=(P("walk", None, None), P("walk", "vec", None), P("walk", None)),
        check_vma=False,
    )
```

```python
import functools

import jax
import jax.numpy as jnp
from jax import lax
from jax.experimental import pallas as pl
from jax.experimental.pallas import tpu as pltpu
from jax.sharding import PartitionSpec as P

MESH = pl.DeviceIdType.MESH
LANES = 128
DEEP = 4
UNIT = 32
GROUP = 2
SKEW = 3
AHEAD = 3
X_SLOW = (16, 100)
X_FAST = 2
X_HUB = (16, 17, 18, 19, 20, 21, 23, 24, 25, 25)
X_LEAF = (3, 5, 7, 8, 10, 11, 12, 14, 15, 16)
Y_LAG = 3
LOAD_LAG = 2
CATCH_UP = 2
Z_HUB = (16, 35)
Z_LEAF = (5, 32)
Z_LAG = 3
Z_LAG_Y = 3
NEAR = 41
RELAY = 22
RELAY_LAG = 5
DIRECT = (2, 1, 4)
DIRECT_WRAP = 3
WRAP_START = 8
WRAP_STEPS = 4
SPAN = 8


def flip(index):
    return index + 1 - 2 * lax.rem(index, 2)


def clip(value, low, high):
    return jnp.minimum(jnp.maximum(value, low), high)


def step_kernel(
    n_walk, n_vec, owners, chol, walkers, table, partner, beyond,
    home, away, up, down, mat, hold, state, acc, result, note, told,
    home_sem, away_sem, up_sem, down_sem,
    mate_send, across_send, relay_send, up_send, down_send,
    x_send, y_send, d_send, r_send, zy_send, zd_send, zr_send, z_send, direct_send, hold_send, hold_sem,
    x_sem, y_sem, d_sem, r_sem, z_sem, zy_sem, zd_sem, zr_sem,
    load_sem, note_send, note_sem, t_send, t_sem,
):
    walk, vec = lax.axis_index("walk"), lax.axis_index("vec")
    rows = n_walk // 2
    last = rows - 1
    row, col = walk // 2, lax.rem(walk, 2)
    low = lax.rem(vec, 2)
    hub = low == col
    leaf = jnp.logical_not(hub)
    pieces, electrons = home.shape[0], home.shape[1]
    blocks = pieces // DEEP
    per_dev = walkers.shape[0]
    quarter = walkers.shape[1] // n_vec
    units = quarter // UNIT
    groups = [(first, min(GROUP, units - first)) for first in range(0, units, GROUP)]
    ends = [first + size for first, size in groups]
    flip_walk, flip_vec = flip(walk), flip(vec)
    far_vec = lax.rem(vec + 2, n_vec)
    z_next = lax.rem(row + 1 - 2 * col + rows, rows)
    order = jnp.where(col == 0, row, last - row)
    order_own = last - order
    z_own = lax.rem(row + 2 * col - 1 + rows, rows)
    direct_to = {"walk": z_own * 2 + col, "vec": vec}
    z_to = {"walk": z_next * 2 + col, "vec": vec}
    across = {"walk": flip_walk, "vec": vec}
    mate = {"walk": walk, "vec": flip_vec}
    over = {"walk": walk, "vec": far_vec}
    above = {"walk": walk + 2, "vec": vec}
    below = {"walk": walk - 2, "vec": vec}
    row_up, row_down = lax.rem(row + 1, rows), lax.rem(row + rows - 1, rows)

    place = col * n_vec + vec
    readers = [({"walk": walk, "vec": lax.rem(vec + j, n_vec)}, place) for j in range(1, n_vec)]
    readers += [({"walk": flip_walk, "vec": lax.rem(vec + j, n_vec)}, place) for j in range(n_vec)]
    readers += [({"walk": row_up * 2, "vec": lax.rem(vec + j, n_vec)}, place + 2 * n_vec) for j in range(n_vec)]
    readers += [({"walk": row_down * 2 + 1, "vec": lax.rem(vec + j, n_vec)}, place + 2 * n_vec) for j in range(n_vec)]

    def each(lo, hi, f):
        def body(k, carry):
            f(k)
            return carry
        lax.fori_loop(lo, hi, body, 0)

    def remote(src, dst, send, recv, target):
        return pltpu.make_async_remote_copy(
            src_ref=src, dst_ref=dst, send_sem=send, recv_sem=recv,
            device_id=target, device_id_type=MESH)

    def chol_piece(k):
        b, j = lax.div(k, DEEP), lax.rem(k, DEEP)
        half = DEEP // 2
        at = b * half + jnp.where(j < half, j, j - half + blocks * half)
        return chol.at[0, 0, :, pl.ds(pl.multiple_of(at * LANES, LANES), LANES)]

    def own_to_home(k):
        return pltpu.make_async_copy(chol_piece(k), home.at[k], home_sem.at[k])

    def own_to_mate(k):
        return remote(chol_piece(k), home.at[k], mate_send, home_sem.at[k], mate)

    def own_across(k):
        return remote(chol_piece(k), away.at[k], across_send, away_sem.at[k], across)

    def away_to_mate(k):
        return remote(away.at[k], away.at[k], relay_send, away_sem.at[k], mate)

    def send_up(k):
        return remote(up.at[k], up.at[k], up_send, up_sem.at[k], above)

    def send_down(k):
        return remote(down.at[k], down.at[k], down_send, down_sem.at[k], below)

    def unit_rows(u):
        return pl.ds(pl.multiple_of(vec * quarter + u * UNIT, UNIT), UNIT)

    def x_unit(u):
        at = unit_rows(u)
        return remote(walkers.at[:, at], partner.at[:, at], x_send, x_sem.at[lax.div(u, GROUP)], across)

    def z_unit(u):
        at = unit_rows(u)
        return remote(partner.at[:, at], beyond.at[:, at], z_send.at[u], z_sem.at[lax.div(u, GROUP)], z_to)

    def direct_unit(u):
        at = unit_rows(u)
        return remote(walkers.at[:, at], hold.at[u], direct_send.at[u], hold_sem.at[u], direct_to)

    def relay_unit(u):
        at = unit_rows(u)
        return remote(hold.at[u], beyond.at[:, at], hold_send.at[u], z_sem.at[lax.div(u, GROUP)], across)

    def direct_count(position):
        return jnp.where(position == last, DIRECT_WRAP,
                         jnp.minimum(DIRECT[0] + DIRECT[1] * position, DIRECT[2]))

    def relay_all():
        def one(u):
            direct_unit(u).wait_recv()
            relay_unit(u).start()
        each(0, direct_count(lax.rem(order_own + last, rows)), one)

    def direct_sent(i):
        paced = clip(lax.div(i - WRAP_START + WRAP_STEPS, WRAP_STEPS), 0, DIRECT_WRAP)
        return jnp.where(order_own == last, paced, direct_count(order_own))

    def group(buffer, n, index, send, recv, target):
        first, size = groups[n]
        at = pl.ds(pl.multiple_of(index * quarter + first * UNIT, UNIT), size * UNIT)
        return remote(buffer.at[:, at], buffer.at[:, at], send, recv.at[n], target)

    def load(w):
        src = walkers.at[w] if w < per_dev else partner.at[w - per_dev]
        return pltpu.make_async_copy(src, state.at[w], load_sem.at[w])

    for w in range(per_dev):
        load(w).start()

    @pl.when(hub)
    def _():
        each(0, pieces, lambda k: own_to_home(k).start())

    def code_of(root):
        here = (lax.div(root, 2) == row).astype(jnp.float32)
        under = (lax.div(root, 2) <= row).astype(jnp.float32)
        at_home = (lax.rem(root, 2) == col).astype(jnp.float32)
        return here + 2.0 * under + 4.0 * at_home

    code_mate = jnp.where(low == 0, code_of(owners[0, 1]), code_of(owners[0, 0]))
    code_own = jnp.where(low == 0, code_of(owners[0, 0]), code_of(owners[0, 1]))
    note[...] = jnp.full(note.shape, code_mate, jnp.float32)

    @pl.when(hub)
    def _():
        told[...] = jnp.full(told.shape, code_own, jnp.float32)

    send_note = remote(note, told, note_send, note_sem, mate)

    bar = pltpu.get_barrier_semaphore()
    for target in (
        [t for t, _ in readers[:2 * n_vec - 1]]
        + [{"walk": r * 2 + c, "vec": lax.rem(vec + j, n_vec)}
           for r in (row_up, row_down) for c in range(2) for j in range(n_vec)]
    ):
        pl.semaphore_signal(bar, inc=1, device_id=target, device_id_type=MESH)
    pl.semaphore_wait(bar, 6 * n_vec - 1)

    each(0, direct_sent(0), lambda u: direct_unit(u).start())

    @pl.when(hub)
    def _():
        send_note.start()
        each(0, min(AHEAD, pieces), lambda k: own_to_mate(k).start())
        each(0, units, lambda u: x_unit(u).start())

    @pl.when(leaf)
    def _():
        def x_count(k):
            slow = lax.div(jnp.minimum(k, X_SLOW[0]), X_SLOW[1])
            return jnp.minimum(slow + jnp.maximum(k - X_SLOW[0], 0) * X_FAST, units)

        def start(k):
            own_across(k).start()
            each(x_count(k), x_count(k + 1), lambda u: x_unit(u).start())
        each(0, pieces, start)
        each(x_count(pieces), units, lambda u: x_unit(u).start())

    acc[...] = jnp.zeros_like(acc)

    @pl.when(leaf)
    def _():
        send_note.wait_recv()

    code = jnp.max(told[...])
    from_home = code >= 4.0
    code = jnp.where(from_home, code - 4.0, code)
    below_or_here = code >= 2.0
    here = jnp.where(below_or_here, code - 2.0, code) >= 1.0
    total = pieces + SKEW * last
    depth = jnp.maximum(row, last - row)

    skip = direct_count(order)

    def sent(i):
        gone = jnp.where(
            hub,
            lax.div(jnp.maximum(i - Z_HUB[0], 0) * (units - skip), Z_HUB[1] - Z_HUB[0]),
            lax.div(jnp.maximum(i - Z_LEAF[0], 0) * (units - skip), Z_LEAF[1] - Z_LEAF[0]))
        return jnp.minimum(skip + gone, units)

    def chain(i):
        @pl.when(i < pieces)
        def _():
            @pl.when(hub)
            def _():
                own_across(i).wait_recv()
                away_to_mate(i).start()

                @pl.when(i + AHEAD < pieces)
                def _():
                    own_to_mate(i + AHEAD).start()

                own_to_home(i).wait()

            @pl.when(leaf)
            def _():
                own_to_mate(i).wait_recv()
                away_to_mate(i).wait_recv()

        ku = i - SKEW * row
        kd = i - SKEW * (last - row)

        @pl.when(jnp.logical_and(ku >= 0, ku < pieces))
        def _():
            own = jnp.where(from_home, home[ku], away[ku])

            @pl.when(row == 0)
            def _():
                up[ku] = own

            @pl.when(row > 0)
            def _():
                send_up(ku).wait_recv()
                up[ku] = jnp.where(here, own, up[ku])

            @pl.when(row < last)
            def _():
                send_up(ku).start()

        @pl.when(jnp.logical_and(kd >= 0, kd < pieces))
        def _():
            own = jnp.where(from_home, home[kd], away[kd])

            @pl.when(row == last)
            def _():
                down[kd] = own

            @pl.when(row < last)
            def _():
                send_down(kd).wait_recv()
                down[kd] = jnp.where(here, own, down[kd])

            @pl.when(row > 0)
            def _():
                send_down(kd).start()

        done = i - SKEW * depth

        @pl.when(jnp.logical_and(done >= 0, done < pieces))
        def _():
            mat[done] = jnp.where(below_or_here, up[done], down[done])

    load_at = X_HUB[-1] + Y_LAG + LOAD_LAG

    def arrive(n):
        group(partner, n, vec, x_send, x_sem, across).wait_recv()
        group(partner, n, vec, y_send, y_sem, over).start()
        group(partner, n, vec, d_send, d_sem, mate).start()

    def pass_on(n):
        group(partner, n, far_vec, y_send, y_sem, over).wait_recv()
        group(partner, n, far_vec, r_send, r_sem, mate).start()

    def load_partner():
        for n in range(len(groups)):
            group(partner, n, vec, d_send, d_sem, mate).wait_recv()
            group(partner, n, vec, r_send, r_sem, mate).wait_recv()
        for w in range(per_dev):
            load(per_dev + w).start()

    def loaded(first):
        for w in range(per_dev):
            load(first + w).wait()

    def z_arrive(n):
        group(beyond, n, vec, zy_send, z_sem, z_to).wait_recv()
        group(beyond, n, vec, zy_send, zy_sem, over).start()
        group(beyond, n, vec, zd_send, zd_sem, mate).start()

    def z_pass_on(n):
        group(beyond, n, far_vec, zy_send, zy_sem, over).wait_recv()
        group(beyond, n, far_vec, zr_send, zr_sem, mate).start()

    half = DEEP // 2
    wide = half * LANES

    def multiply(b, w):
        p = state[w, pl.ds(pl.multiple_of(b * wide, wide), wide), :]
        re = jnp.concatenate([mat[b * DEEP + j] for j in range(half)], axis=1)
        im = jnp.concatenate([mat[b * DEEP + half + j] for j in range(half)], axis=1)
        x = jnp.dot(re, p, preferred_element_type=jnp.float32)
        y = jnp.dot(im, p, preferred_element_type=jnp.float32)
        acc[w, :, :electrons] += x[:, :electrons] - y[:, electrons:]
        acc[w, :, electrons:] += x[:, electrons:] + y[:, :electrons]

    def products(i):
        e = i - SKEW * depth - (DEEP - 1)
        def own_count(e, w):
            return clip(lax.div(e + DEEP - w, DEEP), 0, blocks)

        def partner_count(i, w):
            e = i - SKEW * depth - (DEEP - 1)
            full = clip(lax.div(e + DEEP, DEEP), 0, blocks)
            return jnp.where(i > total, blocks, clip((i - load_at - 2) * CATCH_UP, 0, full))

        spans = [(own_count(e - 1, w), own_count(e, w)) for w in range(per_dev)]
        spans += [(partner_count(i - 1, w), partner_count(i, w)) for w in range(per_dev)]
        def some(w, carry):
            lo, hi = spans[-1]
            for v in range(len(spans) - 1):
                lo = jnp.where(w == v, spans[v][0], lo)
                hi = jnp.where(w == v, spans[v][1], hi)
            lax.fori_loop(lo, hi, lambda b, c: (multiply(b, w), c)[1], 0)
            return carry
        lax.fori_loop(0, len(spans), some, 0)

    sub = lax.broadcasted_iota(jnp.int32, result.shape, 0)
    lane = lax.broadcasted_iota(jnp.int32, result.shape, 1)
    result[...] = jnp.zeros_like(result)
    orbitals = blocks * wide

    def finish(w):
        o = state[w, orbitals:, :]
        m = acc[w].astype(jnp.bfloat16)
        u = jnp.dot(m[:, :electrons], o, preferred_element_type=jnp.float32)
        v = jnp.dot(m[:, electrons:], o, preferred_element_type=jnp.float32)
        g_re = u[:, :electrons] - v[:, electrons:]
        g_im = u[:, electrons:] + v[:, :electrons]
        t_re, t_im = g_re.T, g_im.T
        eye = (lax.broadcasted_iota(jnp.int32, g_re.shape, 0)
               == lax.broadcasted_iota(jnp.int32, g_re.shape, 1))
        values = [
            jnp.sum(jnp.where(eye, g_re, 0.0)),
            jnp.sum(jnp.where(eye, g_im, 0.0)),
            jnp.sum(g_re * t_re - g_im * t_im),
            2.0 * jnp.sum(g_re * t_im),
        ]
        for n, value in enumerate(values):
            result[...] = jnp.where(jnp.logical_and(sub == w, lane == n), value, result[...])

    def tell(n):
        target, where = readers[n]
        return remote(result, table.at[where], t_send.at[n], t_sem.at[where], target)

    def tell_all():
        for n in range(len(readers)):
            tell(n).start()

    events, rest = [], []
    for times, z_times, role in ((X_HUB, Z_HUB, hub), (X_LEAF, Z_LEAF, leaf)):
        late = []
        for n, end in enumerate(ends):
            at = times[min(n, len(times) - 1)]
            events.append((at, role, functools.partial(arrive, n)))
            events.append((at + Y_LAG, role, functools.partial(pass_on, n)))
            fewest = min(DIRECT[0], DIRECT_WRAP)
            span = z_times[1] - z_times[0]
            at = z_times[0] + -(-max(end - fewest, 0) * span // (units - fewest)) + Z_LAG
            if groups[n][0] < max(DIRECT[2], DIRECT_WRAP):
                at = max(at, RELAY + RELAY_LAG)
            for run, when in ((z_arrive, at), (z_pass_on, at + Z_LAG_Y)):
                if when < min(total, NEAR):
                    events.append((when, role, functools.partial(run, n)))
                else:
                    late.append((run, n))
        late.sort(key=lambda item: item[1] + (1 if item[0] is z_pass_on else 0))
        rest.append((role, late))
    events.append((RELAY, None, functools.partial(relay_all)))
    events.append((load_at, None, functools.partial(load_partner)))
    events.append((load_at + 2, None, functools.partial(loaded, per_dev)))
    events.append((min(DEEP - 1 + SKEW * (rows // 2), total), None, functools.partial(loaded, 0)))

    def handle(start, stop):
        for role, late in rest:
            @pl.when(role)
            def _():
                for run, n in late[start:stop]:
                    run(n)

    after = [
        lambda: each(sent(total - 1), units, lambda u: z_unit(u).start()),
        functools.partial(handle, 0, 1),
        lambda: each(total, total + 2, products),
    ]
    for w in range(2 * per_dev):
        after.append(functools.partial(handle, w + 1, w + 2))
        after.append(functools.partial(finish, w))
    after.append(tell_all)
    after.append(functools.partial(handle, 2 * per_dev + 1, 10 * len(groups)))

    families = {}
    for when, role, run in events:
        families.setdefault((run.func, when // SPAN) if role is not None else None, []).append((when, role, run))

    def step(i):
        chain(i)
        for members in families.values():
            times = [when for when, _, _ in members]

            @pl.when(jnp.logical_and(i >= min(times), i <= max(times)))
            def _():
                for when, role, run in members:
                    pl.when(i == when if role is None else jnp.logical_and(i == when, role))(run)
        each(jnp.where(i == 0, direct_sent(0), direct_sent(i - 1)), direct_sent(i), lambda u: direct_unit(u).start())
        each(sent(i - 1), sent(i), lambda u: z_unit(u).start())
        products(i)

    each(0, total, step)
    for run in after:
        run()

    table[place] = result[...]

    for n in range(len(groups)):
        group(beyond, n, vec, zd_send, zd_sem, mate).wait_recv()
        group(beyond, n, vec, zr_send, zr_sem, mate).wait_recv()

    def all_sent(buffer, send, target):
        remote(buffer, buffer, send, t_sem.at[0], target).wait_send()

    @pl.when(hub)
    def _():
        send_note.wait_send()
        all_sent(home, mate_send, mate)
        all_sent(away, relay_send, mate)

    @pl.when(leaf)
    def _():
        all_sent(away, across_send, across)

    @pl.when(row < last)
    def _():
        all_sent(up, up_send, above)

    @pl.when(row > 0)
    def _():
        all_sent(down, down_send, below)

    part = partner.at[:, pl.ds(pl.multiple_of(vec * quarter, UNIT), quarter)]
    for send, target in (
        (x_send, across), (y_send, over), (d_send, mate), (r_send, mate),
        (zy_send, over), (zd_send, mate), (zr_send, mate),
    ):
        all_sent(part, send, target)

    each(skip, units, lambda u: z_unit(u).wait_send())
    each(0, direct_count(order_own), lambda u: direct_unit(u).wait_send())
    each(0, direct_count(lax.rem(order_own + last, rows)), lambda u: relay_unit(u).wait_send())

    for n in range(len(readers)):
        tell(n).wait_send()

    for j in range(1, n_vec):
        v = lax.rem(vec + j, n_vec)
        remote(result, table.at[0], t_send.at[0], t_sem.at[col * n_vec + v], mate).wait_recv()
    for j in range(n_vec):
        remote(result, table.at[0], t_send.at[0], t_sem.at[(1 - col) * n_vec + j], mate).wait_recv()
    for j in range(2 * n_vec):
        remote(result, table.at[0], t_send.at[0], t_sem.at[2 * n_vec + j], mate).wait_recv()


def step_all(n_walk, n_vec, owners, chol, walkers):
    per_dev, height, width = walkers.shape
    electrons, orbitals = chol.shape[2:]
    pieces = orbitals // LANES
    units = height // n_vec // UNIT
    groups = -(-units // GROUP)
    big = pltpu.VMEM((pieces, electrons, LANES), chol.dtype)
    dma = pltpu.SemaphoreType.DMA
    any_spec = pl.BlockSpec(memory_space=pl.ANY)
    smem = pl.BlockSpec(memory_space=pltpu.SMEM)
    same = jax.ShapeDtypeStruct(walkers.shape, walkers.dtype)
    return pl.pallas_call(
        functools.partial(step_kernel, n_walk, n_vec),
        out_shape=(jax.ShapeDtypeStruct((4 * n_vec, 8, 128), jnp.float32), same, same),
        in_specs=[smem, any_spec, any_spec],
        out_specs=(pl.BlockSpec(memory_space=pltpu.VMEM), any_spec, any_spec),
        scratch_shapes=[
            big, big, big, big, big,
            pltpu.VMEM((max(DIRECT[2], DIRECT_WRAP), per_dev, UNIT, width), walkers.dtype),
            pltpu.VMEM((2 * per_dev, height, width), walkers.dtype),
            pltpu.VMEM((2 * per_dev, electrons, width), jnp.float32),
            pltpu.VMEM((8, 128), jnp.float32),
            pltpu.VMEM((8, 128), jnp.float32),
            pltpu.VMEM((8, 128), jnp.float32),
        ] + [dma((pieces,))] * 4 + [dma] * 12 + [dma((units,))] * 4 + [dma((groups,))] * 8
        + [dma((2 * per_dev,)), dma, dma, dma((4 * n_vec - 1,)), dma((4 * n_vec,))],
        compiler_params=pltpu.CompilerParams(
            collective_id=0, has_side_effects=True, vmem_limit_bytes=62 * 1024 * 1024),
        name="step_all",
    )(owners, chol, walkers)


BITS = 4


def branch_kernel(
    n_walk, n_vec, slots, walkers, partner, beyond, table,
    branched, bias, energy, held, facts, in_sem, out_sem, t_sem,
):
    walk, vec = lax.axis_index("walk"), lax.axis_index("vec")
    col = lax.rem(walk, 2)
    per_dev, height = walkers.shape[:2]
    piece = height // BITS
    total = per_dev * n_walk

    def rows(t):
        return pl.ds(t * piece, piece)

    def fetch(buffer, w, s, t):
        return pltpu.make_async_copy(buffer.at[w, rows(t)], held.at[s, rows(t)], in_sem.at[s, t])

    def put(s, t):
        return pltpu.make_async_copy(held.at[s, rows(t)], branched.at[s, rows(t)], out_sem.at[s, t])

    cases = [(s, t) for s in range(per_dev) for t in range(BITS)]
    picks = []
    for s in range(per_dev):
        relative = lax.rem(slots[s] - (walk - 1) * per_dev + total, total)
        side, w = lax.div(relative, per_dev), lax.rem(relative, per_dev)
        mine, beside = side == 1, side == 2 * (1 - col)
        far = jnp.logical_not(jnp.logical_or(mine, beside))
        picks.append((w, jnp.where(far, 1, 0), jnp.where(mine, col, 1 - col)))
        for wanted, buffer in ((mine, walkers), (beside, partner), (far, beyond)):
            @pl.when(wanted)
            def _():
                for t in range(BITS):
                    fetch(buffer, w, s, t).start()
    facts_in = pltpu.make_async_copy(table, facts, t_sem)
    facts_in.start()
    for s, t in cases:
        fetch(walkers, 0, s, t).wait()
        put(s, t).start()
    facts_in.wait()

    for s, (w, far, block) in enumerate(picks):
        def value(v, g, lane):
            sender = lax.rem(v, 2)
            at = far * 2 * n_vec + sender * n_vec + lax.div(v, 2) * 2 + g
            return facts[at, jnp.where(block == sender, 0, per_dev) + w, lane]

        for g in range(2):
            for part in range(2):
                bias[s, g, part] = value(vec, g, part)
        for part in range(2):
            energy[s, part] = -0.5 * sum(value(jnp.int32(v), g, 2 + part) for v in range(n_vec) for g in range(2))

    for s, t in cases:
        put(s, t).wait()


def branch(n_walk, n_vec, slots, walkers, partner, beyond, table):
    per_dev = walkers.shape[0]
    dma = pltpu.SemaphoreType.DMA
    any_spec = pl.BlockSpec(memory_space=pl.ANY)
    smem = pl.BlockSpec(memory_space=pltpu.SMEM)
    return pl.pallas_call(
        functools.partial(branch_kernel, n_walk, n_vec),
        out_shape=(
            jax.ShapeDtypeStruct(walkers.shape, walkers.dtype),
            jax.ShapeDtypeStruct((per_dev, 2, 2), jnp.float32),
            jax.ShapeDtypeStruct((per_dev, 2), jnp.float32),
        ),
        in_specs=[smem, any_spec, any_spec, any_spec, any_spec],
        out_specs=(any_spec, smem, smem),
        scratch_shapes=[
            pltpu.VMEM(walkers.shape, walkers.dtype), pltpu.SMEM(table.shape, table.dtype),
            dma((per_dev, BITS)), dma((per_dev, BITS)), dma,
        ],
        compiler_params=pltpu.CompilerParams(vmem_limit_bytes=62 * 1024 * 1024),
        name="branch",
    )(slots, walkers, partner, beyond, table)


def shards(n_walk, n_vec, walkers, chol, owners, branch_src):
    table, partner, beyond = step_all(n_walk, n_vec, owners, chol, walkers)
    return branch(n_walk, n_vec, branch_src, walkers, partner, beyond, table)


def solution(mesh):
    n_walk, n_vec = mesh.shape["walk"], mesh.shape["vec"]
    return jax.shard_map(
        functools.partial(shards, n_walk, n_vec),
        mesh=mesh,
        in_specs=(P("walk", None, None), P("vec", "walk", None, None), P("vec", None), P("walk")),
        out_specs=(P("walk", None, None), P("walk", "vec", None), P("walk", None)),
        check_vma=False,
    )
```

```python
import functools

import jax
import jax.numpy as jnp
from jax import lax
from jax.experimental import pallas as pl
from jax.experimental.pallas import tpu as pltpu
from jax.sharding import PartitionSpec as P

MESH = pl.DeviceIdType.MESH
LANES = 128
DEEP = 4
UNIT = 32
GROUP = 2
SKEW = 3
AHEAD = 8
BATCH = 4
X_SLOW = (16, 100)
X_FAST = 2
X_HUB = (16, 17, 18, 19, 20, 21, 23, 24, 25, 25)
X_LEAF = (3, 5, 7, 8, 10, 11, 12, 14, 15, 16)
Y_LAG = 3
LOAD_LAG = 2
CATCH_UP = 2
Z_HUB = (16, 33)
Z_LEAF = (5, 32)
Z_LAG = 3
Z_LAG_Y = 3
NEAR = 41
RELAY = 22
RELAY_LAG = 5
DIRECT = (2, 1, 4)
DIRECT_WRAP = 3
WRAP_START = 4
WRAP_STEPS = 2
SPAN = 8


def flip(index):
    return index + 1 - 2 * lax.rem(index, 2)


def clip(value, low, high):
    return jnp.minimum(jnp.maximum(value, low), high)


def step_kernel(
    n_walk, n_vec, owners, chol, walkers, table, partner, beyond,
    home, away, up, down, mat, hold, state, acc, result, note, told,
    home_sem, away_sem, up_sem, down_sem,
    mate_send, across_send, relay_send, up_send, down_send,
    x_send, y_send, d_send, r_send, zy_send, zd_send, zr_send, z_send, direct_send, hold_send, hold_sem,
    x_sem, y_sem, z_sem, zy_sem, d_sem, r_sem, zd_sem, zr_sem,
    load_sem, keep_sem, note_send, note_sem, t_send, t_sem,
):
    walk, vec = lax.axis_index("walk"), lax.axis_index("vec")
    rows = n_walk // 2
    last = rows - 1
    row, col = walk // 2, lax.rem(walk, 2)
    low = lax.rem(vec, 2)
    hub = low == col
    leaf = jnp.logical_not(hub)
    pieces, electrons = home.shape[0], home.shape[1]
    blocks = pieces // DEEP
    per_dev = walkers.shape[0]
    quarter = walkers.shape[1] // n_vec
    units = quarter // UNIT
    groups = [(first, min(GROUP, units - first)) for first in range(0, units, GROUP)]
    ends = [first + size for first, size in groups]
    flip_walk, flip_vec = flip(walk), flip(vec)
    far_vec = lax.rem(vec + 2, n_vec)
    z_next = lax.rem(row + 1 - 2 * col + rows, rows)
    order = jnp.where(col == 0, row, last - row)
    order_own = last - order
    z_own = lax.rem(row + 2 * col - 1 + rows, rows)
    direct_to = {"walk": z_own * 2 + col, "vec": vec}
    z_to = {"walk": z_next * 2 + col, "vec": vec}
    across = {"walk": flip_walk, "vec": vec}
    mate = {"walk": walk, "vec": flip_vec}
    over = {"walk": walk, "vec": far_vec}
    above = {"walk": walk + 2, "vec": vec}
    below = {"walk": walk - 2, "vec": vec}
    row_up, row_down = lax.rem(row + 1, rows), lax.rem(row + rows - 1, rows)

    place = col * n_vec + vec
    readers = [({"walk": walk, "vec": lax.rem(vec + j, n_vec)}, place) for j in range(1, n_vec)]
    readers += [({"walk": flip_walk, "vec": lax.rem(vec + j, n_vec)}, place) for j in range(n_vec)]
    readers += [({"walk": row_up * 2, "vec": lax.rem(vec + j, n_vec)}, place + 2 * n_vec) for j in range(n_vec)]
    readers += [({"walk": row_down * 2 + 1, "vec": lax.rem(vec + j, n_vec)}, place + 2 * n_vec) for j in range(n_vec)]

    def each(lo, hi, f):
        def body(k, carry):
            f(k)
            return carry
        lax.fori_loop(lo, hi, body, 0)

    def remote(src, dst, send, recv, target):
        return pltpu.make_async_remote_copy(
            src_ref=src, dst_ref=dst, send_sem=send, recv_sem=recv,
            device_id=target, device_id_type=MESH)

    def chol_piece(k):
        b, j = lax.div(k, DEEP), lax.rem(k, DEEP)
        half = DEEP // 2
        at = b * half + jnp.where(j < half, j, j - half + blocks * half)
        return chol.at[0, 0, :, pl.ds(pl.multiple_of(at * LANES, LANES), LANES)]

    def own_to_home(k):
        return pltpu.make_async_copy(chol_piece(k), home.at[k], home_sem.at[lax.div(k, BATCH)])

    def home_batch(k):
        return home.at[pl.ds(k, BATCH)]

    def own_to_mate(k):
        return remote(chol_piece(k), home.at[k], mate_send, home_sem.at[lax.div(k, BATCH)], mate)

    def own_across(k):
        return remote(chol_piece(k), away.at[k], across_send, away_sem.at[k], across)

    def away_to_mate(k):
        return remote(away.at[k], away.at[k], relay_send, away_sem.at[k], mate)

    def send_up(k):
        return remote(up.at[k], up.at[k], up_send, up_sem.at[k], above)

    def send_down(k):
        return remote(down.at[k], down.at[k], down_send, down_sem.at[k], below)

    def unit_rows(u):
        return pl.ds(pl.multiple_of(vec * quarter + u * UNIT, UNIT), UNIT)

    def x_unit(u):
        at = unit_rows(u)
        return remote(walkers.at[:, at], partner.at[:, at], x_send, x_sem.at[lax.div(u, GROUP)], across)

    def z_unit(u):
        at = unit_rows(u)
        return remote(partner.at[:, at], beyond.at[:, at], z_send, z_sem.at[lax.div(u, GROUP)], z_to)

    def direct_unit(u):
        at = unit_rows(u)
        return remote(walkers.at[:, at], hold.at[u], direct_send.at[u], hold_sem.at[u], direct_to)

    def relay_unit(u):
        at = unit_rows(u)
        return remote(hold.at[u], beyond.at[:, at], hold_send.at[u], z_sem.at[lax.div(u, GROUP)], across)

    def direct_count(position):
        return jnp.where(position == last, DIRECT_WRAP,
                         jnp.minimum(DIRECT[0] + DIRECT[1] * position, DIRECT[2]))

    def relay_all():
        def one(u):
            direct_unit(u).wait_recv()
            relay_unit(u).start()
        each(0, direct_count(lax.rem(order_own + last, rows)), one)

    def direct_sent(i):
        paced = clip(lax.div(i - WRAP_START + WRAP_STEPS, WRAP_STEPS), 0, DIRECT_WRAP)
        return jnp.where(order_own == last, paced, direct_count(order_own))

    def group(buffer, n, index, send, recv, target):
        first, size = groups[n]
        at = pl.ds(pl.multiple_of(index * quarter + first * UNIT, UNIT), size * UNIT)
        return remote(buffer.at[:, at], buffer.at[:, at], send, recv, target)

    def quarter_of(buffer, send, recv):
        at = pl.ds(pl.multiple_of(vec * quarter, UNIT), quarter)
        return remote(buffer.at[:, at], buffer.at[:, at], send, recv, mate)

    def load(w):
        src = walkers.at[w] if w < per_dev else partner.at[w - per_dev]
        return pltpu.make_async_copy(src, state.at[w], load_sem.at[w])

    bar = pltpu.get_barrier_semaphore()
    for target in (
        [t for t, _ in readers[:2 * n_vec - 1]]
        + [{"walk": r * 2 + c, "vec": lax.rem(vec + j, n_vec)}
           for r in (row_up, row_down) for c in range(2) for j in range(n_vec)]
    ):
        pl.semaphore_signal(bar, inc=1, device_id=target, device_id_type=MESH)
    for w in range(per_dev):
        load(w).start()

    @pl.when(hub)
    def _():
        each(0, pieces, lambda k: own_to_home(k).start())

    def code_of(root):
        here = (lax.div(root, 2) == row).astype(jnp.float32)
        under = (lax.div(root, 2) <= row).astype(jnp.float32)
        at_home = (lax.rem(root, 2) == col).astype(jnp.float32)
        return here + 2.0 * under + 4.0 * at_home

    code_mate = jnp.where(low == 0, code_of(owners[0, 1]), code_of(owners[0, 0]))
    code_own = jnp.where(low == 0, code_of(owners[0, 0]), code_of(owners[0, 1]))
    note[...] = jnp.full(note.shape, code_mate, jnp.float32)

    @pl.when(hub)
    def _():
        told[...] = jnp.full(told.shape, code_own, jnp.float32)

    send_note = remote(note, told, note_send, note_sem, mate)

    pl.semaphore_wait(bar, 6 * n_vec - 1)

    each(0, direct_sent(0), lambda u: direct_unit(u).start())

    @pl.when(hub)
    def _():
        send_note.start()
        each(0, min(AHEAD, pieces), lambda k: own_to_mate(k).start())
        each(0, units, lambda u: x_unit(u).start())

    @pl.when(leaf)
    def _():
        def x_count(k):
            slow = lax.div(jnp.minimum(k, X_SLOW[0]), X_SLOW[1])
            return jnp.minimum(slow + jnp.maximum(k - X_SLOW[0], 0) * X_FAST, units)

        def start(k):
            own_across(k).start()
            each(x_count(k), x_count(k + 1), lambda u: x_unit(u).start())
        each(0, pieces, start)
        each(x_count(pieces), units, lambda u: x_unit(u).start())

    acc[...] = jnp.zeros_like(acc)

    @pl.when(leaf)
    def _():
        send_note.wait_recv()

    code = jnp.max(told[...])
    from_home = code >= 4.0
    code = jnp.where(from_home, code - 4.0, code)
    below_or_here = code >= 2.0
    here = jnp.where(below_or_here, code - 2.0, code) >= 1.0
    total = pieces + SKEW * last
    depth = jnp.maximum(row, last - row)

    skip = direct_count(order)

    def sent(i):
        gone = jnp.where(
            hub,
            lax.div(jnp.maximum(i - Z_HUB[0], 0) * (units - skip), Z_HUB[1] - Z_HUB[0]),
            lax.div(jnp.maximum(i - Z_LEAF[0], 0) * (units - skip), Z_LEAF[1] - Z_LEAF[0]))
        return jnp.minimum(skip + gone, units)

    def chain(i):
        @pl.when(i < pieces)
        def _():
            @pl.when(hub)
            def _():
                own_across(i).wait_recv()
                away_to_mate(i).start()

                @pl.when(i + AHEAD < pieces)
                def _():
                    own_to_mate(i + AHEAD).start()

                @pl.when(lax.rem(i, BATCH) == 0)
                def _():
                    pltpu.make_async_copy(home_batch(i), home_batch(i), home_sem.at[lax.div(i, BATCH)]).wait()

            @pl.when(leaf)
            def _():
                @pl.when(lax.rem(i, BATCH) == 0)
                def _():
                    remote(home_batch(i), home_batch(i), mate_send, home_sem.at[lax.div(i, BATCH)], mate).wait_recv()

                away_to_mate(i).wait_recv()

        ku = i - SKEW * row
        kd = i - SKEW * (last - row)

        @pl.when(jnp.logical_and(ku >= 0, ku < pieces))
        def _():
            own = jnp.where(from_home, home[ku], away[ku])

            @pl.when(row == 0)
            def _():
                up[ku] = own

            @pl.when(row > 0)
            def _():
                send_up(ku).wait_recv()
                up[ku] = jnp.where(here, own, up[ku])

            @pl.when(row < last)
            def _():
                send_up(ku).start()

        @pl.when(jnp.logical_and(kd >= 0, kd < pieces))
        def _():
            own = jnp.where(from_home, home[kd], away[kd])

            @pl.when(row == last)
            def _():
                down[kd] = own

            @pl.when(row < last)
            def _():
                send_down(kd).wait_recv()
                down[kd] = jnp.where(here, own, down[kd])

            @pl.when(row > 0)
            def _():
                send_down(kd).start()

        done = i - SKEW * depth

        @pl.when(jnp.logical_and(done >= 0, done < pieces))
        def _():
            mat[done] = jnp.where(below_or_here, up[done], down[done])

    load_at = X_HUB[-1] + Y_LAG + LOAD_LAG

    def arrive(n):
        group(partner, n, vec, x_send, x_sem.at[n], across).wait_recv()
        group(partner, n, vec, y_send, y_sem.at[n], over).start()
        group(partner, n, vec, d_send, d_sem, mate).start()

    def pass_on(n):
        group(partner, n, far_vec, y_send, y_sem.at[n], over).wait_recv()
        group(partner, n, far_vec, r_send, r_sem, mate).start()

    def load_partner():
        quarter_of(partner, d_send, d_sem).wait_recv()
        quarter_of(partner, r_send, r_sem).wait_recv()
        for w in range(per_dev):
            load(per_dev + w).start()

    def loaded(first):
        for w in range(per_dev):
            load(first + w).wait()

    def z_arrive(n):
        group(beyond, n, vec, zy_send, z_sem.at[n], z_to).wait_recv()
        group(beyond, n, vec, zy_send, zy_sem.at[n], over).start()
        group(beyond, n, vec, zd_send, zd_sem, mate).start()

    def z_pass_on(n):
        group(beyond, n, far_vec, zy_send, zy_sem.at[n], over).wait_recv()
        group(beyond, n, far_vec, zr_send, zr_sem, mate).start()

    half = DEEP // 2
    wide = half * LANES

    def multiply(b, w):
        p = state[w, pl.ds(pl.multiple_of(b * wide, wide), wide), :]
        re = jnp.concatenate([mat[b * DEEP + j] for j in range(half)], axis=1)
        im = jnp.concatenate([mat[b * DEEP + half + j] for j in range(half)], axis=1)
        x = jnp.dot(re, p, preferred_element_type=jnp.float32)
        y = jnp.dot(im, p, preferred_element_type=jnp.float32)
        acc[w, :, :electrons] += x[:, :electrons] - y[:, electrons:]
        acc[w, :, electrons:] += x[:, electrons:] + y[:, :electrons]

    def products(i):
        e = i - SKEW * depth - (DEEP - 1)
        def own_count(e, w):
            return clip(lax.div(e + DEEP - w, DEEP), 0, blocks)

        def partner_count(i, w):
            e = i - SKEW * depth - (DEEP - 1)
            full = clip(lax.div(e + DEEP, DEEP), 0, blocks)
            return jnp.where(i > total, blocks, clip((i - load_at - 2) * CATCH_UP, 0, full))

        spans = [(own_count(e - 1, w), own_count(e, w)) for w in range(per_dev)]
        spans += [(partner_count(i - 1, w), partner_count(i, w)) for w in range(per_dev)]
        def some(w, carry):
            lo, hi = spans[-1]
            for v in range(len(spans) - 1):
                lo = jnp.where(w == v, spans[v][0], lo)
                hi = jnp.where(w == v, spans[v][1], hi)
            lax.fori_loop(lo, hi, lambda b, c: (multiply(b, w), c)[1], 0)
            return carry
        lax.fori_loop(0, len(spans), some, 0)

    sub = lax.broadcasted_iota(jnp.int32, result.shape, 0)
    lane = lax.broadcasted_iota(jnp.int32, result.shape, 1)
    result[...] = jnp.zeros_like(result)
    orbitals = blocks * wide

    def finish(w):
        o = state[w, orbitals:, :]
        m = acc[w].astype(jnp.bfloat16)
        u = jnp.dot(m[:, :electrons], o, preferred_element_type=jnp.float32)
        v = jnp.dot(m[:, electrons:], o, preferred_element_type=jnp.float32)
        g_re = u[:, :electrons] - v[:, electrons:]
        g_im = u[:, electrons:] + v[:, :electrons]
        t_re, t_im = g_re.T, g_im.T
        eye = (lax.broadcasted_iota(jnp.int32, g_re.shape, 0)
               == lax.broadcasted_iota(jnp.int32, g_re.shape, 1))
        values = [
            jnp.sum(jnp.where(eye, g_re, 0.0)),
            jnp.sum(jnp.where(eye, g_im, 0.0)),
            jnp.sum(g_re * t_re - g_im * t_im),
            2.0 * jnp.sum(g_re * t_im),
        ]
        for n, value in enumerate(values):
            result[...] = jnp.where(jnp.logical_and(sub == w, lane == n), value, result[...])

    def tell(n):
        target, where = readers[n]
        return remote(result, table.at[where], t_send, t_sem, target)

    keep = pltpu.make_async_copy(result, table.at[place], keep_sem)

    def tell_all():
        for n in range(len(readers)):
            tell(n).start()
        keep.start()

    events, rest = [], []
    for times, z_times, role in ((X_HUB, Z_HUB, hub), (X_LEAF, Z_LEAF, leaf)):
        late = []
        for n, end in enumerate(ends):
            at = times[min(n, len(times) - 1)]
            events.append((at, role, functools.partial(arrive, n)))
            events.append((at + Y_LAG, role, functools.partial(pass_on, n)))
            fewest = min(DIRECT[0], DIRECT_WRAP)
            span = z_times[1] - z_times[0]
            at = z_times[0] + -(-max(end - fewest, 0) * span // (units - fewest)) + Z_LAG
            if groups[n][0] < max(DIRECT[2], DIRECT_WRAP):
                at = max(at, RELAY + RELAY_LAG)
            for run, when in ((z_arrive, at), (z_pass_on, at + Z_LAG_Y)):
                if when < min(total, NEAR):
                    events.append((when, role, functools.partial(run, n)))
                else:
                    late.append((run, n))
        late.sort(key=lambda item: item[1] + (1 if item[0] is z_pass_on else 0))
        rest.append((role, late))
    events.append((RELAY, None, functools.partial(relay_all)))
    events.append((load_at, None, functools.partial(load_partner)))
    events.append((load_at + 2, None, functools.partial(loaded, per_dev)))
    events.append((min(DEEP - 1 + SKEW * (rows // 2), total), None, functools.partial(loaded, 0)))

    def handle(start, stop):
        for role, late in rest:
            @pl.when(role)
            def _():
                for run, n in late[start:stop]:
                    run(n)

    after = [
        lambda: each(sent(total - 1), units, lambda u: z_unit(u).start()),
        functools.partial(handle, 0, 1),
        lambda: each(total, total + 2, products),
    ]
    for w in range(2 * per_dev):
        after.append(functools.partial(handle, w + 1, w + 2))
        after.append(functools.partial(finish, w))
    after.append(tell_all)
    after.append(functools.partial(handle, 2 * per_dev + 1, 10 * len(groups)))

    families = {}
    for when, role, run in events:
        families.setdefault((run.func, when // SPAN) if role is not None else None, []).append((when, role, run))

    def step(i):
        chain(i)
        for members in families.values():
            times = [when for when, _, _ in members]

            @pl.when(jnp.logical_and(i >= min(times), i <= max(times)))
            def _():
                for when, role, run in members:
                    pl.when(i == when if role is None else jnp.logical_and(i == when, role))(run)
        each(jnp.where(i == 0, direct_sent(0), direct_sent(i - 1)), direct_sent(i), lambda u: direct_unit(u).start())
        each(sent(i - 1), sent(i), lambda u: z_unit(u).start())
        products(i)

    each(0, total, step)
    for run in after:
        run()


    quarter_of(beyond, zd_send, zd_sem).wait_recv()
    quarter_of(beyond, zr_send, zr_sem).wait_recv()

    def all_sent(buffer, send, target):
        remote(buffer, buffer, send, t_sem, target).wait_send()

    @pl.when(hub)
    def _():
        send_note.wait_send()
        all_sent(home, mate_send, mate)
        all_sent(away, relay_send, mate)

    @pl.when(leaf)
    def _():
        all_sent(away, across_send, across)

    @pl.when(row < last)
    def _():
        all_sent(up, up_send, above)

    @pl.when(row > 0)
    def _():
        all_sent(down, down_send, below)

    part = partner.at[:, pl.ds(pl.multiple_of(vec * quarter, UNIT), quarter)]
    for send, target in (
        (x_send, across), (y_send, over), (d_send, mate), (r_send, mate),
        (zy_send, over), (zd_send, mate), (zr_send, mate),
    ):
        all_sent(part, send, target)

    keep.wait()
    for count in range(min(DIRECT[0], DIRECT_WRAP), max(DIRECT[2], DIRECT_WRAP) + 1):
        @pl.when(skip == count)
        def _():
            some = partner.at[:, pl.ds(0, (units - count) * UNIT)]
            all_sent(some, z_send, z_to)

    each(0, direct_count(order_own), lambda u: direct_unit(u).wait_send())
    each(0, direct_count(lax.rem(order_own + last, rows)), lambda u: relay_unit(u).wait_send())

    heard = table.at[pl.ds(0, len(readers))]
    remote(heard, heard, t_send, t_sem, mate).wait_send()

    remote(heard, heard, t_send, t_sem, mate).wait_recv()


def step_all(n_walk, n_vec, owners, chol, walkers):
    per_dev, height, width = walkers.shape
    electrons, orbitals = chol.shape[2:]
    pieces = orbitals // LANES
    units = height // n_vec // UNIT
    groups = -(-units // GROUP)
    most = max(DIRECT[2], DIRECT_WRAP)
    big = pltpu.VMEM((pieces, electrons, LANES), chol.dtype)
    dma = pltpu.SemaphoreType.DMA
    any_spec = pl.BlockSpec(memory_space=pl.ANY)
    smem = pl.BlockSpec(memory_space=pltpu.SMEM)
    same = jax.ShapeDtypeStruct(walkers.shape, walkers.dtype)
    return pl.pallas_call(
        functools.partial(step_kernel, n_walk, n_vec),
        out_shape=(jax.ShapeDtypeStruct((4 * n_vec, 8, 128), jnp.float32), same, same),
        in_specs=[smem, any_spec, any_spec],
        out_specs=(any_spec, any_spec, any_spec),
        scratch_shapes=[
            big, big, big, big, big,
            pltpu.VMEM((max(DIRECT[2], DIRECT_WRAP), per_dev, UNIT, width), walkers.dtype),
            pltpu.VMEM((2 * per_dev, height, width), walkers.dtype),
            pltpu.VMEM((2 * per_dev, electrons, width), jnp.float32),
            pltpu.VMEM((8, 128), jnp.float32),
            pltpu.VMEM((8, 128), jnp.float32),
            pltpu.VMEM((8, 128), jnp.float32),
        ] + [dma((-(-pieces // BATCH),))] + [dma((pieces,))] * 3 + [dma] * 12 + [dma] + [dma((most,))] * 3 + [dma((groups,))] * 4 + [dma] * 4
        + [dma((2 * per_dev,)), dma, dma, dma, dma, dma],
        compiler_params=pltpu.CompilerParams(
            collective_id=0, has_side_effects=True, vmem_limit_bytes=62 * 1024 * 1024),
        name="step_all",
    )(owners, chol, walkers)


BITS = 4


def branch_kernel(
    n_walk, n_vec, slots, walkers, partner, beyond, table,
    branched, bias, energy, held, facts, in_sem, out_sem, t_sem,
):
    walk, vec = lax.axis_index("walk"), lax.axis_index("vec")
    col = lax.rem(walk, 2)
    per_dev, height = walkers.shape[:2]
    piece = height // BITS
    total = per_dev * n_walk

    def rows(t):
        return pl.ds(t * piece, piece)

    def fetch(buffer, w, s, t):
        return pltpu.make_async_copy(buffer.at[w, rows(t)], held.at[s, rows(t)], in_sem.at[s, t])

    def put(s, t):
        return pltpu.make_async_copy(held.at[s, rows(t)], branched.at[s, rows(t)], out_sem.at[s, t])

    cases = [(s, t) for s in range(per_dev) for t in range(BITS)]
    picks = []
    for s in range(per_dev):
        relative = lax.rem(slots[s] - (walk - 1) * per_dev + total, total)
        side, w = lax.div(relative, per_dev), lax.rem(relative, per_dev)
        mine, beside = side == 1, side == 2 * (1 - col)
        far = jnp.logical_not(jnp.logical_or(mine, beside))
        picks.append((w, jnp.where(far, 1, 0), jnp.where(mine, col, 1 - col)))
        for wanted, buffer in ((mine, walkers), (beside, partner), (far, beyond)):
            @pl.when(wanted)
            def _():
                for t in range(BITS):
                    fetch(buffer, w, s, t).start()
    facts_in = pltpu.make_async_copy(table, facts, t_sem)
    facts_in.start()
    for s, t in cases:
        fetch(walkers, 0, s, t).wait()
        put(s, t).start()
    facts_in.wait()

    for s, (w, far, block) in enumerate(picks):
        def value(v, g, lane):
            sender = lax.rem(v, 2)
            at = far * 2 * n_vec + sender * n_vec + lax.div(v, 2) * 2 + g
            return facts[at, jnp.where(block == sender, 0, per_dev) + w, lane]

        for g in range(2):
            for part in range(2):
                bias[s, g, part] = value(vec, g, part)
        for part in range(2):
            energy[s, part] = -0.5 * sum(value(jnp.int32(v), g, 2 + part) for v in range(n_vec) for g in range(2))

    for s, t in cases:
        put(s, t).wait()


def branch(n_walk, n_vec, slots, walkers, partner, beyond, table):
    per_dev = walkers.shape[0]
    dma = pltpu.SemaphoreType.DMA
    any_spec = pl.BlockSpec(memory_space=pl.ANY)
    smem = pl.BlockSpec(memory_space=pltpu.SMEM)
    return pl.pallas_call(
        functools.partial(branch_kernel, n_walk, n_vec),
        out_shape=(
            jax.ShapeDtypeStruct(walkers.shape, walkers.dtype),
            jax.ShapeDtypeStruct((per_dev, 2, 2), jnp.float32),
            jax.ShapeDtypeStruct((per_dev, 2), jnp.float32),
        ),
        in_specs=[smem, any_spec, any_spec, any_spec, any_spec],
        out_specs=(any_spec, smem, smem),
        scratch_shapes=[
            pltpu.VMEM(walkers.shape, walkers.dtype), pltpu.SMEM(table.shape, table.dtype),
            dma((per_dev, BITS)), dma((per_dev, BITS)), dma,
        ],
        compiler_params=pltpu.CompilerParams(vmem_limit_bytes=62 * 1024 * 1024),
        name="branch",
    )(slots, walkers, partner, beyond, table)


def shards(n_walk, n_vec, walkers, chol, owners, branch_src):
    table, partner, beyond = step_all(n_walk, n_vec, owners, chol, walkers)
    return branch(n_walk, n_vec, branch_src, walkers, partner, beyond, table)


def solution(mesh):
    n_walk, n_vec = mesh.shape["walk"], mesh.shape["vec"]
    return jax.shard_map(
        functools.partial(shards, n_walk, n_vec),
        mesh=mesh,
        in_specs=(P("walk", None, None), P("vec", "walk", None, None), P("vec", None), P("walk")),
        out_specs=(P("walk", None, None), P("walk", "vec", None), P("walk", None)),
        check_vma=False,
    )
```

```python
import functools

import jax
import jax.numpy as jnp
from jax import lax
from jax.experimental import pallas as pl
from jax.experimental.pallas import tpu as pltpu
from jax.sharding import PartitionSpec as P

MESH = pl.DeviceIdType.MESH
LANES = 128
DEEP = 4
UNIT = 32
GROUP = 2
SKEW = 3
AHEAD = 8
BATCH = 4
X_SLOW = (17, 100)
X_FAST = 2
X_HUB = (16, 17, 18, 19, 20, 21, 23, 24, 25, 25)
X_LEAF = (6, 7, 9, 10, 12, 13, 14, 16, 17, 18)
Y_LAG = 3
LOAD_LAG = 2
CATCH_UP = 1
Z_HUB = (16, 33)
Z_LEAF = (8, 34)
HUB_START = 3
Z_LAG = 4
Z_LAG_Y = 3
NEAR = 41
RELAY = 22
RELAY_LAG = 5
DIRECT = (2, 1, 4)
DIRECT_WRAP = 3
WRAP_START = 4
WRAP_STEPS = 2
SPAN = 8


def flip(index):
    return index + 1 - 2 * lax.rem(index, 2)


def clip(value, low, high):
    return jnp.minimum(jnp.maximum(value, low), high)


def step_kernel(
    n_walk, n_vec, owners, chol, walkers, table, partner, beyond,
    home, away, up, down, mat, hold, state, acc, result, note, told,
    home_sem, away_sem, up_sem, down_sem,
    mate_send, across_send, relay_send, up_send, down_send,
    x_send, y_send, d_send, r_send, zy_send, zd_send, zr_send, z_send, direct_send, hold_send, hold_sem,
    x_sem, y_sem, z_sem, zy_sem, d_sem, r_sem, zd_sem, zr_sem,
    load_sem, keep_sem, note_send, note_sem, t_send, t_sem,
):
    walk, vec = lax.axis_index("walk"), lax.axis_index("vec")
    rows = n_walk // 2
    last = rows - 1
    row, col = walk // 2, lax.rem(walk, 2)
    low = lax.rem(vec, 2)
    hub = low == col
    leaf = jnp.logical_not(hub)
    pieces, electrons = home.shape[0], home.shape[1]
    blocks = pieces // DEEP
    per_dev = walkers.shape[0]
    quarter = walkers.shape[1] // n_vec
    units = quarter // UNIT
    groups = [(first, min(GROUP, units - first)) for first in range(0, units, GROUP)]
    ends = [first + size for first, size in groups]
    flip_walk, flip_vec = flip(walk), flip(vec)
    far_vec = lax.rem(vec + 2, n_vec)
    z_next = lax.rem(row + 1 - 2 * col + rows, rows)
    order = jnp.where(col == 0, row, last - row)
    order_own = last - order
    z_own = lax.rem(row + 2 * col - 1 + rows, rows)
    direct_to = {"walk": z_own * 2 + col, "vec": vec}
    z_to = {"walk": z_next * 2 + col, "vec": vec}
    across = {"walk": flip_walk, "vec": vec}
    mate = {"walk": walk, "vec": flip_vec}
    over = {"walk": walk, "vec": far_vec}
    above = {"walk": walk + 2, "vec": vec}
    below = {"walk": walk - 2, "vec": vec}
    row_up, row_down = lax.rem(row + 1, rows), lax.rem(row + rows - 1, rows)

    place = col * n_vec + vec
    readers = [({"walk": walk, "vec": lax.rem(vec + j, n_vec)}, place) for j in range(1, n_vec)]
    readers += [({"walk": flip_walk, "vec": lax.rem(vec + j, n_vec)}, place) for j in range(n_vec)]
    readers += [({"walk": row_up * 2, "vec": lax.rem(vec + j, n_vec)}, place + 2 * n_vec) for j in range(n_vec)]
    readers += [({"walk": row_down * 2 + 1, "vec": lax.rem(vec + j, n_vec)}, place + 2 * n_vec) for j in range(n_vec)]

    def each(lo, hi, f):
        def body(k, carry):
            f(k)
            return carry
        lax.fori_loop(lo, hi, body, 0)

    def remote(src, dst, send, recv, target):
        return pltpu.make_async_remote_copy(
            src_ref=src, dst_ref=dst, send_sem=send, recv_sem=recv,
            device_id=target, device_id_type=MESH)

    def chol_piece(k):
        b, j = lax.div(k, DEEP), lax.rem(k, DEEP)
        half = DEEP // 2
        at = b * half + jnp.where(j < half, j, j - half + blocks * half)
        return chol.at[0, 0, :, pl.ds(pl.multiple_of(at * LANES, LANES), LANES)]

    def own_to_home(k):
        return pltpu.make_async_copy(chol_piece(k), home.at[k], home_sem.at[lax.div(k, BATCH)])

    def home_batch(k):
        return home.at[pl.ds(k, BATCH)]

    def own_to_mate(k):
        return remote(chol_piece(k), home.at[k], mate_send, home_sem.at[lax.div(k, BATCH)], mate)

    def own_across(k):
        return remote(chol_piece(k), away.at[k], across_send, away_sem.at[k], across)

    def away_to_mate(k):
        return remote(away.at[k], away.at[k], relay_send, away_sem.at[k], mate)

    def send_up(k):
        return remote(up.at[k], up.at[k], up_send, up_sem.at[k], above)

    def send_down(k):
        return remote(down.at[k], down.at[k], down_send, down_sem.at[k], below)

    def unit_rows(u):
        return pl.ds(pl.multiple_of(vec * quarter + u * UNIT, UNIT), UNIT)

    def x_unit(u):
        at = unit_rows(u)
        return remote(walkers.at[:, at], partner.at[:, at], x_send, x_sem.at[lax.div(u, GROUP)], across)

    def z_unit(u):
        at = unit_rows(u)
        return remote(partner.at[:, at], beyond.at[:, at], z_send, z_sem.at[lax.div(u, GROUP)], z_to)

    def direct_unit(u):
        at = unit_rows(u)
        return remote(walkers.at[:, at], hold.at[u], direct_send.at[u], hold_sem.at[u], direct_to)

    def relay_unit(u):
        at = unit_rows(u)
        return remote(hold.at[u], beyond.at[:, at], hold_send.at[u], z_sem.at[lax.div(u, GROUP)], across)

    def direct_count(position):
        return jnp.where(position == last, DIRECT_WRAP,
                         jnp.minimum(DIRECT[0] + DIRECT[1] * position, DIRECT[2]))

    def relay_all():
        def one(u):
            direct_unit(u).wait_recv()
            relay_unit(u).start()
        each(0, direct_count(lax.rem(order_own + last, rows)), one)

    def direct_sent(i):
        paced = clip(lax.div(i - WRAP_START + WRAP_STEPS, WRAP_STEPS), 0, DIRECT_WRAP)
        return jnp.where(order_own == last, paced, direct_count(order_own))

    def group(buffer, n, index, send, recv, target):
        first, size = groups[n]
        at = pl.ds(pl.multiple_of(index * quarter + first * UNIT, UNIT), size * UNIT)
        return remote(buffer.at[:, at], buffer.at[:, at], send, recv, target)

    def quarter_of(buffer, send, recv):
        at = pl.ds(pl.multiple_of(vec * quarter, UNIT), quarter)
        return remote(buffer.at[:, at], buffer.at[:, at], send, recv, mate)

    def load(w):
        src = walkers.at[w] if w < per_dev else partner.at[w - per_dev]
        return pltpu.make_async_copy(src, state.at[w], load_sem.at[w])

    bar = pltpu.get_barrier_semaphore()
    for target in (
        [t for t, _ in readers[:2 * n_vec - 1]]
        + [{"walk": r * 2 + c, "vec": lax.rem(vec + j, n_vec)}
           for r in (row_up, row_down) for c in range(2) for j in range(n_vec)]
    ):
        pl.semaphore_signal(bar, inc=1, device_id=target, device_id_type=MESH)
    for w in range(per_dev):
        load(w).start()

    @pl.when(hub)
    def _():
        each(0, pieces, lambda k: own_to_home(k).start())

    def code_of(root):
        here = (lax.div(root, 2) == row).astype(jnp.float32)
        under = (lax.div(root, 2) <= row).astype(jnp.float32)
        at_home = (lax.rem(root, 2) == col).astype(jnp.float32)
        return here + 2.0 * under + 4.0 * at_home

    code_mate = jnp.where(low == 0, code_of(owners[0, 1]), code_of(owners[0, 0]))
    code_own = jnp.where(low == 0, code_of(owners[0, 0]), code_of(owners[0, 1]))
    note[...] = jnp.full(note.shape, code_mate, jnp.float32)

    @pl.when(hub)
    def _():
        told[...] = jnp.full(told.shape, code_own, jnp.float32)

    send_note = remote(note, told, note_send, note_sem, mate)

    pl.semaphore_wait(bar, 6 * n_vec - 1)

    each(0, direct_sent(0), lambda u: direct_unit(u).start())

    @pl.when(hub)
    def _():
        send_note.start()
        each(0, min(AHEAD, pieces), lambda k: own_to_mate(k).start())

    @pl.when(leaf)
    def _():
        def x_count(k):
            slow = lax.div(jnp.minimum(k, X_SLOW[0]), X_SLOW[1])
            return jnp.minimum(slow + jnp.maximum(k - X_SLOW[0], 0) * X_FAST, units)

        def start(k):
            own_across(k).start()
            each(x_count(k), x_count(k + 1), lambda u: x_unit(u).start())
        each(0, pieces, start)
        each(x_count(pieces), units, lambda u: x_unit(u).start())

    acc[...] = jnp.zeros_like(acc)

    @pl.when(leaf)
    def _():
        send_note.wait_recv()

    code = jnp.max(told[...])
    from_home = code >= 4.0
    code = jnp.where(from_home, code - 4.0, code)
    below_or_here = code >= 2.0
    here = jnp.where(below_or_here, code - 2.0, code) >= 1.0
    total = pieces + SKEW * last
    depth = jnp.maximum(row, last - row)

    skip = direct_count(order)

    def sent(i):
        gone = jnp.where(
            hub,
            lax.div(jnp.maximum(i - Z_HUB[0], 0) * (units - skip), Z_HUB[1] - Z_HUB[0]),
            lax.div(jnp.maximum(i - Z_LEAF[0], 0) * (units - skip), Z_LEAF[1] - Z_LEAF[0]))
        return jnp.minimum(skip + gone, units)

    def chain(i):
        @pl.when(i < pieces)
        def _():
            @pl.when(hub)
            def _():
                own_across(i).wait_recv()
                away_to_mate(i).start()

                @pl.when(i + AHEAD < pieces)
                def _():
                    own_to_mate(i + AHEAD).start()

                @pl.when(lax.rem(i, BATCH) == 0)
                def _():
                    pltpu.make_async_copy(home_batch(i), home_batch(i), home_sem.at[lax.div(i, BATCH)]).wait()

            @pl.when(leaf)
            def _():
                @pl.when(lax.rem(i, BATCH) == 0)
                def _():
                    remote(home_batch(i), home_batch(i), mate_send, home_sem.at[lax.div(i, BATCH)], mate).wait_recv()

                away_to_mate(i).wait_recv()

        ku = i - SKEW * row
        kd = i - SKEW * (last - row)

        @pl.when(jnp.logical_and(ku >= 0, ku < pieces))
        def _():
            own = jnp.where(from_home, home[ku], away[ku])

            @pl.when(row == 0)
            def _():
                up[ku] = own

            @pl.when(row > 0)
            def _():
                send_up(ku).wait_recv()
                up[ku] = jnp.where(here, own, up[ku])

            @pl.when(row < last)
            def _():
                send_up(ku).start()

        @pl.when(jnp.logical_and(kd >= 0, kd < pieces))
        def _():
            own = jnp.where(from_home, home[kd], away[kd])

            @pl.when(row == last)
            def _():
                down[kd] = own

            @pl.when(row < last)
            def _():
                send_down(kd).wait_recv()
                down[kd] = jnp.where(here, own, down[kd])

            @pl.when(row > 0)
            def _():
                send_down(kd).start()

        done = i - SKEW * depth

        @pl.when(jnp.logical_and(done >= 0, done < pieces))
        def _():
            mat[done] = jnp.where(below_or_here, up[done], down[done])

    load_at = X_HUB[-1] + Y_LAG + LOAD_LAG

    def arrive(n):
        group(partner, n, vec, x_send, x_sem.at[n], across).wait_recv()
        group(partner, n, vec, y_send, y_sem.at[n], over).start()
        group(partner, n, vec, d_send, d_sem, mate).start()

    def pass_on(n):
        group(partner, n, far_vec, y_send, y_sem.at[n], over).wait_recv()
        group(partner, n, far_vec, r_send, r_sem, mate).start()

    def load_partner():
        quarter_of(partner, d_send, d_sem).wait_recv()
        quarter_of(partner, r_send, r_sem).wait_recv()
        for w in range(per_dev):
            load(per_dev + w).start()

    def loaded(first):
        for w in range(per_dev):
            load(first + w).wait()

    def z_arrive(n):
        group(beyond, n, vec, zy_send, z_sem.at[n], z_to).wait_recv()
        group(beyond, n, vec, zy_send, zy_sem.at[n], over).start()
        group(beyond, n, vec, zd_send, zd_sem, mate).start()

    def z_pass_on(n):
        group(beyond, n, far_vec, zy_send, zy_sem.at[n], over).wait_recv()
        group(beyond, n, far_vec, zr_send, zr_sem, mate).start()

    half = DEEP // 2
    wide = half * LANES

    def multiply(b, w):
        p = state[w, pl.ds(pl.multiple_of(b * wide, wide), wide), :]
        re = jnp.concatenate([mat[b * DEEP + j] for j in range(half)], axis=1)
        im = jnp.concatenate([mat[b * DEEP + half + j] for j in range(half)], axis=1)
        x = jnp.dot(re, p, preferred_element_type=jnp.float32)
        y = jnp.dot(im, p, preferred_element_type=jnp.float32)
        acc[w, :, :electrons] += x[:, :electrons] - y[:, electrons:]
        acc[w, :, electrons:] += x[:, electrons:] + y[:, :electrons]

    def products(i):
        e = i - SKEW * depth - (DEEP - 1)
        def own_count(e, w):
            return clip(lax.div(e + DEEP - w, DEEP), 0, blocks)

        def partner_count(i, w):
            e = i - SKEW * depth - (DEEP - 1)
            full = clip(lax.div(e + DEEP, DEEP), 0, blocks)
            return jnp.where(i > total, blocks, clip((i - load_at - 2) * CATCH_UP, 0, full))

        spans = [(own_count(e - 1, w), own_count(e, w)) for w in range(per_dev)]
        spans += [(partner_count(i - 1, w), partner_count(i, w)) for w in range(per_dev)]
        def some(w, carry):
            lo, hi = spans[-1]
            for v in range(len(spans) - 1):
                lo = jnp.where(w == v, spans[v][0], lo)
                hi = jnp.where(w == v, spans[v][1], hi)
            lax.fori_loop(lo, hi, lambda b, c: (multiply(b, w), c)[1], 0)
            return carry
        lax.fori_loop(0, len(spans), some, 0)

    sub = lax.broadcasted_iota(jnp.int32, result.shape, 0)
    lane = lax.broadcasted_iota(jnp.int32, result.shape, 1)
    result[...] = jnp.zeros_like(result)
    orbitals = blocks * wide

    def finish(w):
        o = state[w, orbitals:, :]
        m = acc[w].astype(jnp.bfloat16)
        u = jnp.dot(m[:, :electrons], o, preferred_element_type=jnp.float32)
        v = jnp.dot(m[:, electrons:], o, preferred_element_type=jnp.float32)
        g_re = u[:, :electrons] - v[:, electrons:]
        g_im = u[:, electrons:] + v[:, :electrons]
        t_re, t_im = g_re.T, g_im.T
        eye = (lax.broadcasted_iota(jnp.int32, g_re.shape, 0)
               == lax.broadcasted_iota(jnp.int32, g_re.shape, 1))
        values = [
            jnp.sum(jnp.where(eye, g_re, 0.0)),
            jnp.sum(jnp.where(eye, g_im, 0.0)),
            jnp.sum(g_re * t_re - g_im * t_im),
            2.0 * jnp.sum(g_re * t_im),
        ]
        for n, value in enumerate(values):
            result[...] = jnp.where(jnp.logical_and(sub == w, lane == n), value, result[...])

    def tell(n):
        target, where = readers[n]
        return remote(result, table.at[where], t_send, t_sem, target)

    keep = pltpu.make_async_copy(result, table.at[place], keep_sem)

    def tell_all():
        for n in range(len(readers)):
            tell(n).start()
        keep.start()

    def hub_units():
        each(0, units, lambda u: x_unit(u).start())

    events, rest = [], []
    events.append((HUB_START, hub, functools.partial(hub_units)))
    for times, z_times, role in ((X_HUB, Z_HUB, hub), (X_LEAF, Z_LEAF, leaf)):
        late = []
        for n, end in enumerate(ends):
            at = times[min(n, len(times) - 1)]
            events.append((at, role, functools.partial(arrive, n)))
            events.append((at + Y_LAG, role, functools.partial(pass_on, n)))
            fewest = min(DIRECT[0], DIRECT_WRAP)
            span = z_times[1] - z_times[0]
            at = z_times[0] + -(-max(end - fewest, 0) * span // (units - fewest)) + Z_LAG
            if groups[n][0] < max(DIRECT[2], DIRECT_WRAP):
                at = max(at, RELAY + RELAY_LAG)
            for run, when in ((z_arrive, at), (z_pass_on, at + Z_LAG_Y)):
                if when < min(total, NEAR):
                    events.append((when, role, functools.partial(run, n)))
                else:
                    late.append((run, n))
        late.sort(key=lambda item: item[1] + (1 if item[0] is z_pass_on else 0))
        rest.append((role, late))
    events.append((RELAY, None, functools.partial(relay_all)))
    events.append((load_at, None, functools.partial(load_partner)))
    events.append((load_at + 2, None, functools.partial(loaded, per_dev)))
    events.append((min(DEEP - 1 + SKEW * (rows // 2), total), None, functools.partial(loaded, 0)))

    def handle(start, stop):
        for role, late in rest:
            @pl.when(role)
            def _():
                for run, n in late[start:stop]:
                    run(n)

    after = [
        lambda: each(sent(total - 1), units, lambda u: z_unit(u).start()),
        functools.partial(handle, 0, 1),
        lambda: each(total, total + 2, products),
    ]
    for w in range(2 * per_dev):
        after.append(functools.partial(handle, w + 1, w + 2))
        after.append(functools.partial(finish, w))
    after.append(tell_all)
    after.append(functools.partial(handle, 2 * per_dev + 1, 10 * len(groups)))

    families = {}
    for when, role, run in events:
        families.setdefault((run.func, when // SPAN) if role is not None else None, []).append((when, role, run))

    def step(i):
        chain(i)
        for members in families.values():
            times = [when for when, _, _ in members]

            @pl.when(jnp.logical_and(i >= min(times), i <= max(times)))
            def _():
                for when, role, run in members:
                    pl.when(i == when if role is None else jnp.logical_and(i == when, role))(run)
        each(jnp.where(i == 0, direct_sent(0), direct_sent(i - 1)), direct_sent(i), lambda u: direct_unit(u).start())
        each(sent(i - 1), sent(i), lambda u: z_unit(u).start())
        products(i)

    each(0, total, step)
    for run in after:
        run()


    quarter_of(beyond, zd_send, zd_sem).wait_recv()
    quarter_of(beyond, zr_send, zr_sem).wait_recv()

    def all_sent(buffer, send, target):
        remote(buffer, buffer, send, t_sem, target).wait_send()

    @pl.when(hub)
    def _():
        send_note.wait_send()
        all_sent(home, mate_send, mate)
        all_sent(away, relay_send, mate)

    @pl.when(leaf)
    def _():
        all_sent(away, across_send, across)

    @pl.when(row < last)
    def _():
        all_sent(up, up_send, above)

    @pl.when(row > 0)
    def _():
        all_sent(down, down_send, below)

    part = partner.at[:, pl.ds(pl.multiple_of(vec * quarter, UNIT), quarter)]
    for send, target in (
        (x_send, across), (y_send, over), (d_send, mate), (r_send, mate),
        (zy_send, over), (zd_send, mate), (zr_send, mate),
    ):
        all_sent(part, send, target)

    keep.wait()
    for count in range(min(DIRECT[0], DIRECT_WRAP), max(DIRECT[2], DIRECT_WRAP) + 1):
        @pl.when(skip == count)
        def _():
            some = partner.at[:, pl.ds(0, (units - count) * UNIT)]
            all_sent(some, z_send, z_to)

    each(0, direct_count(order_own), lambda u: direct_unit(u).wait_send())
    each(0, direct_count(lax.rem(order_own + last, rows)), lambda u: relay_unit(u).wait_send())

    heard = table.at[pl.ds(0, len(readers))]
    remote(heard, heard, t_send, t_sem, mate).wait_send()

    remote(heard, heard, t_send, t_sem, mate).wait_recv()


def step_all(n_walk, n_vec, owners, chol, walkers):
    per_dev, height, width = walkers.shape
    electrons, orbitals = chol.shape[2:]
    pieces = orbitals // LANES
    units = height // n_vec // UNIT
    groups = -(-units // GROUP)
    most = max(DIRECT[2], DIRECT_WRAP)
    big = pltpu.VMEM((pieces, electrons, LANES), chol.dtype)
    dma = pltpu.SemaphoreType.DMA
    any_spec = pl.BlockSpec(memory_space=pl.ANY)
    smem = pl.BlockSpec(memory_space=pltpu.SMEM)
    same = jax.ShapeDtypeStruct(walkers.shape, walkers.dtype)
    return pl.pallas_call(
        functools.partial(step_kernel, n_walk, n_vec),
        out_shape=(jax.ShapeDtypeStruct((4 * n_vec, 8, 128), jnp.float32), same, same),
        in_specs=[smem, any_spec, any_spec],
        out_specs=(any_spec, any_spec, any_spec),
        scratch_shapes=[
            big, big, big, big, big,
            pltpu.VMEM((max(DIRECT[2], DIRECT_WRAP), per_dev, UNIT, width), walkers.dtype),
            pltpu.VMEM((2 * per_dev, height, width), walkers.dtype),
            pltpu.VMEM((2 * per_dev, electrons, width), jnp.float32),
            pltpu.VMEM((8, 128), jnp.float32),
            pltpu.VMEM((8, 128), jnp.float32),
            pltpu.VMEM((8, 128), jnp.float32),
        ] + [dma((-(-pieces // BATCH),))] + [dma((pieces,))] * 3 + [dma] * 12 + [dma] + [dma((most,))] * 3 + [dma((groups,))] * 4 + [dma] * 4
        + [dma((2 * per_dev,)), dma, dma, dma, dma, dma],
        compiler_params=pltpu.CompilerParams(
            collective_id=0, has_side_effects=True, vmem_limit_bytes=62 * 1024 * 1024),
        name="step_all",
    )(owners, chol, walkers)


BITS = 4


def branch_kernel(
    n_walk, n_vec, slots, walkers, partner, beyond, table,
    branched, bias, energy, held, facts, in_sem, out_sem, t_sem,
):
    walk, vec = lax.axis_index("walk"), lax.axis_index("vec")
    col = lax.rem(walk, 2)
    per_dev, height = walkers.shape[:2]
    piece = height // BITS
    total = per_dev * n_walk

    def rows(t):
        return pl.ds(t * piece, piece)

    def fetch(buffer, w, s, t):
        return pltpu.make_async_copy(buffer.at[w, rows(t)], held.at[s, rows(t)], in_sem.at[s, t])

    def put(s, t):
        return pltpu.make_async_copy(held.at[s, rows(t)], branched.at[s, rows(t)], out_sem.at[s, t])

    cases = [(s, t) for s in range(per_dev) for t in range(BITS)]
    picks = []
    for s in range(per_dev):
        relative = lax.rem(slots[s] - (walk - 1) * per_dev + total, total)
        side, w = lax.div(relative, per_dev), lax.rem(relative, per_dev)
        mine, beside = side == 1, side == 2 * (1 - col)
        far = jnp.logical_not(jnp.logical_or(mine, beside))
        picks.append((w, jnp.where(far, 1, 0), jnp.where(mine, col, 1 - col)))
        for wanted, buffer in ((mine, walkers), (beside, partner), (far, beyond)):
            @pl.when(wanted)
            def _():
                for t in range(BITS):
                    fetch(buffer, w, s, t).start()
    facts_in = pltpu.make_async_copy(table, facts, t_sem)
    facts_in.start()
    for s, t in cases:
        fetch(walkers, 0, s, t).wait()
        put(s, t).start()
    facts_in.wait()

    for s, (w, far, block) in enumerate(picks):
        def value(v, g, lane):
            sender = lax.rem(v, 2)
            at = far * 2 * n_vec + sender * n_vec + lax.div(v, 2) * 2 + g
            return facts[at, jnp.where(block == sender, 0, per_dev) + w, lane]

        for g in range(2):
            for part in range(2):
                bias[s, g, part] = value(vec, g, part)
        for part in range(2):
            energy[s, part] = -0.5 * sum(value(jnp.int32(v), g, 2 + part) for v in range(n_vec) for g in range(2))

    for s, t in cases:
        put(s, t).wait()


def branch(n_walk, n_vec, slots, walkers, partner, beyond, table):
    per_dev = walkers.shape[0]
    dma = pltpu.SemaphoreType.DMA
    any_spec = pl.BlockSpec(memory_space=pl.ANY)
    smem = pl.BlockSpec(memory_space=pltpu.SMEM)
    return pl.pallas_call(
        functools.partial(branch_kernel, n_walk, n_vec),
        out_shape=(
            jax.ShapeDtypeStruct(walkers.shape, walkers.dtype),
            jax.ShapeDtypeStruct((per_dev, 2, 2), jnp.float32),
            jax.ShapeDtypeStruct((per_dev, 2), jnp.float32),
        ),
        in_specs=[smem, any_spec, any_spec, any_spec, any_spec],
        out_specs=(any_spec, smem, smem),
        scratch_shapes=[
            pltpu.VMEM(walkers.shape, walkers.dtype), pltpu.SMEM(table.shape, table.dtype),
            dma((per_dev, BITS)), dma((per_dev, BITS)), dma,
        ],
        compiler_params=pltpu.CompilerParams(vmem_limit_bytes=62 * 1024 * 1024),
        name="branch",
    )(slots, walkers, partner, beyond, table)


def shards(n_walk, n_vec, walkers, chol, owners, branch_src):
    table, partner, beyond = step_all(n_walk, n_vec, owners, chol, walkers)
    return branch(n_walk, n_vec, branch_src, walkers, partner, beyond, table)


def solution(mesh):
    n_walk, n_vec = mesh.shape["walk"], mesh.shape["vec"]
    return jax.shard_map(
        functools.partial(shards, n_walk, n_vec),
        mesh=mesh,
        in_specs=(P("walk", None, None), P("vec", "walk", None, None), P("vec", None), P("walk")),
        out_specs=(P("walk", None, None), P("walk", "vec", None), P("walk", None)),
        check_vma=False,
    )
```

```python
import functools

import jax
import jax.numpy as jnp
from jax import lax
from jax.experimental import pallas as pl
from jax.experimental.pallas import tpu as pltpu
from jax.sharding import PartitionSpec as P

MESH = pl.DeviceIdType.MESH
LANES = 128
DEEP = 4
UNIT = 32
GROUP = 2
SKEW = 3
AHEAD = 8
BATCH = 4
X_SLOW = (17, 100)
X_FAST = 2
X_HUB = (16, 17, 18, 19, 20, 21, 23, 24, 25, 25)
X_LEAF = (4, 6, 8, 9, 11, 12, 13, 15, 16, 17)
Y_LAG = 3
LOAD_LAG = 2
CATCH_UP = 1
Z_HUB = (16, 33)
Z_LEAF = (6, 33)
HUB_START = 0
Z_LAG = 4
Z_LAG_Y = 3
NEAR = 41
RELAY = 22
RELAY_LAG = 5
DIRECT = (2, 1, 4)
DIRECT_WRAP = 3
WRAP_START = 4
WRAP_STEPS = 2
SPAN = 8


def flip(index):
    return index + 1 - 2 * lax.rem(index, 2)


def clip(value, low, high):
    return jnp.minimum(jnp.maximum(value, low), high)


def step_kernel(
    n_walk, n_vec, owners, chol, walkers, table, partner, beyond,
    home, away, up, down, mat, hold, state, acc, result, note, told,
    home_sem, away_sem, up_sem, down_sem,
    mate_send, across_send, relay_send, up_send, down_send,
    x_send, y_send, d_send, r_send, zy_send, zd_send, zr_send, z_send, direct_send, hold_send, hold_sem,
    x_sem, y_sem, z_sem, zy_sem, d_sem, r_sem, zd_sem, zr_sem,
    load_sem, keep_sem, note_send, note_sem, t_send, t_sem,
):
    walk, vec = lax.axis_index("walk"), lax.axis_index("vec")
    rows = n_walk // 2
    last = rows - 1
    row, col = walk // 2, lax.rem(walk, 2)
    low = lax.rem(vec, 2)
    hub = low == col
    leaf = jnp.logical_not(hub)
    pieces, electrons = home.shape[0], home.shape[1]
    blocks = pieces // DEEP
    per_dev = walkers.shape[0]
    quarter = walkers.shape[1] // n_vec
    units = quarter // UNIT
    groups = [(first, min(GROUP, units - first)) for first in range(0, units, GROUP)]
    ends = [first + size for first, size in groups]
    flip_walk, flip_vec = flip(walk), flip(vec)
    far_vec = lax.rem(vec + 2, n_vec)
    z_next = lax.rem(row + 1 - 2 * col + rows, rows)
    order = jnp.where(col == 0, row, last - row)
    order_own = last - order
    z_own = lax.rem(row + 2 * col - 1 + rows, rows)
    direct_to = {"walk": z_own * 2 + col, "vec": vec}
    z_to = {"walk": z_next * 2 + col, "vec": vec}
    across = {"walk": flip_walk, "vec": vec}
    mate = {"walk": walk, "vec": flip_vec}
    over = {"walk": walk, "vec": far_vec}
    above = {"walk": walk + 2, "vec": vec}
    below = {"walk": walk - 2, "vec": vec}
    row_up, row_down = lax.rem(row + 1, rows), lax.rem(row + rows - 1, rows)

    place = col * n_vec + vec
    readers = [({"walk": walk, "vec": lax.rem(vec + j, n_vec)}, place) for j in range(1, n_vec)]
    readers += [({"walk": flip_walk, "vec": lax.rem(vec + j, n_vec)}, place) for j in range(n_vec)]
    readers += [({"walk": row_up * 2, "vec": lax.rem(vec + j, n_vec)}, place + 2 * n_vec) for j in range(n_vec)]
    readers += [({"walk": row_down * 2 + 1, "vec": lax.rem(vec + j, n_vec)}, place + 2 * n_vec) for j in range(n_vec)]

    def each(lo, hi, f):
        def body(k, carry):
            f(k)
            return carry
        lax.fori_loop(lo, hi, body, 0)

    def remote(src, dst, send, recv, target):
        return pltpu.make_async_remote_copy(
            src_ref=src, dst_ref=dst, send_sem=send, recv_sem=recv,
            device_id=target, device_id_type=MESH)

    def chol_piece(k):
        b, j = lax.div(k, DEEP), lax.rem(k, DEEP)
        half = DEEP // 2
        at = b * half + jnp.where(j < half, j, j - half + blocks * half)
        return chol.at[0, 0, :, pl.ds(pl.multiple_of(at * LANES, LANES), LANES)]

    def own_to_home(k):
        return pltpu.make_async_copy(chol_piece(k), home.at[k], home_sem.at[lax.div(k, BATCH)])

    def home_batch(k):
        return home.at[pl.ds(k, BATCH)]

    def own_to_mate(k):
        return remote(chol_piece(k), home.at[k], mate_send, home_sem.at[lax.div(k, BATCH)], mate)

    def own_across(k):
        return remote(chol_piece(k), away.at[k], across_send, away_sem.at[k], across)

    def away_to_mate(k):
        return remote(away.at[k], away.at[k], relay_send, away_sem.at[k], mate)

    def send_up(k):
        return remote(up.at[k], up.at[k], up_send, up_sem.at[k], above)

    def send_down(k):
        return remote(down.at[k], down.at[k], down_send, down_sem.at[k], below)

    def unit_rows(u):
        return pl.ds(pl.multiple_of(vec * quarter + u * UNIT, UNIT), UNIT)

    def x_unit(u):
        at = unit_rows(u)
        return remote(walkers.at[:, at], partner.at[:, at], x_send, x_sem.at[lax.div(u, GROUP)], across)

    def z_unit(u):
        at = unit_rows(u)
        return remote(partner.at[:, at], beyond.at[:, at], z_send, z_sem.at[lax.div(u, GROUP)], z_to)

    def direct_unit(u):
        at = unit_rows(u)
        return remote(walkers.at[:, at], hold.at[u], direct_send.at[u], hold_sem.at[u], direct_to)

    def relay_unit(u):
        at = unit_rows(u)
        return remote(hold.at[u], beyond.at[:, at], hold_send.at[u], z_sem.at[lax.div(u, GROUP)], across)

    def direct_count(position):
        return jnp.where(position == last, DIRECT_WRAP,
                         jnp.minimum(DIRECT[0] + DIRECT[1] * position, DIRECT[2]))

    def relay_all():
        def one(u):
            direct_unit(u).wait_recv()
            relay_unit(u).start()
        each(0, direct_count(lax.rem(order_own + last, rows)), one)

    def direct_sent(i):
        paced = clip(lax.div(i - WRAP_START + WRAP_STEPS, WRAP_STEPS), 0, DIRECT_WRAP)
        return jnp.where(order_own == last, paced, direct_count(order_own))

    def group(buffer, n, index, send, recv, target):
        first, size = groups[n]
        at = pl.ds(pl.multiple_of(index * quarter + first * UNIT, UNIT), size * UNIT)
        return remote(buffer.at[:, at], buffer.at[:, at], send, recv, target)

    def quarter_of(buffer, send, recv):
        at = pl.ds(pl.multiple_of(vec * quarter, UNIT), quarter)
        return remote(buffer.at[:, at], buffer.at[:, at], send, recv, mate)

    def load(w):
        src = walkers.at[w] if w < per_dev else partner.at[w - per_dev]
        return pltpu.make_async_copy(src, state.at[w], load_sem.at[w])

    bar = pltpu.get_barrier_semaphore()
    for target in (
        [t for t, _ in readers[:2 * n_vec - 1]]
        + [{"walk": r * 2 + c, "vec": lax.rem(vec + j, n_vec)}
           for r in (row_up, row_down) for c in range(2) for j in range(n_vec)]
    ):
        pl.semaphore_signal(bar, inc=1, device_id=target, device_id_type=MESH)
    for w in range(per_dev):
        load(w).start()

    @pl.when(hub)
    def _():
        each(0, pieces, lambda k: own_to_home(k).start())

    def code_of(root):
        here = (lax.div(root, 2) == row).astype(jnp.float32)
        under = (lax.div(root, 2) <= row).astype(jnp.float32)
        at_home = (lax.rem(root, 2) == col).astype(jnp.float32)
        return here + 2.0 * under + 4.0 * at_home

    code_mate = jnp.where(low == 0, code_of(owners[0, 1]), code_of(owners[0, 0]))
    code_own = jnp.where(low == 0, code_of(owners[0, 0]), code_of(owners[0, 1]))
    note[...] = jnp.full(note.shape, code_mate, jnp.float32)

    @pl.when(hub)
    def _():
        told[...] = jnp.full(told.shape, code_own, jnp.float32)

    send_note = remote(note, told, note_send, note_sem, mate)

    pl.semaphore_wait(bar, 6 * n_vec - 1)

    each(0, direct_sent(0), lambda u: direct_unit(u).start())

    @pl.when(hub)
    def _():
        send_note.start()
        each(0, min(AHEAD, pieces), lambda k: own_to_mate(k).start())

    @pl.when(leaf)
    def _():
        def x_count(k):
            slow = lax.div(jnp.minimum(k, X_SLOW[0]), X_SLOW[1])
            return jnp.minimum(slow + jnp.maximum(k - X_SLOW[0], 0) * X_FAST, units)

        def start(k):
            own_across(k).start()
            each(x_count(k), x_count(k + 1), lambda u: x_unit(u).start())
        each(0, pieces, start)
        each(x_count(pieces), units, lambda u: x_unit(u).start())

    acc[...] = jnp.zeros_like(acc)

    @pl.when(leaf)
    def _():
        send_note.wait_recv()

    code = jnp.max(told[...])
    from_home = code >= 4.0
    code = jnp.where(from_home, code - 4.0, code)
    below_or_here = code >= 2.0
    here = jnp.where(below_or_here, code - 2.0, code) >= 1.0
    total = pieces + SKEW * last
    depth = jnp.maximum(row, last - row)

    skip = direct_count(order)

    def sent(i):
        gone = jnp.where(
            hub,
            lax.div(jnp.maximum(i - Z_HUB[0], 0) * (units - skip), Z_HUB[1] - Z_HUB[0]),
            lax.div(jnp.maximum(i - Z_LEAF[0], 0) * (units - skip), Z_LEAF[1] - Z_LEAF[0]))
        return jnp.minimum(skip + gone, units)

    def chain(i):
        @pl.when(i < pieces)
        def _():
            @pl.when(hub)
            def _():
                own_across(i).wait_recv()
                away_to_mate(i).start()

                @pl.when(i + AHEAD < pieces)
                def _():
                    own_to_mate(i + AHEAD).start()

                @pl.when(lax.rem(i, BATCH) == 0)
                def _():
                    pltpu.make_async_copy(home_batch(i), home_batch(i), home_sem.at[lax.div(i, BATCH)]).wait()

            @pl.when(leaf)
            def _():
                @pl.when(lax.rem(i, BATCH) == 0)
                def _():
                    remote(home_batch(i), home_batch(i), mate_send, home_sem.at[lax.div(i, BATCH)], mate).wait_recv()

                away_to_mate(i).wait_recv()

        ku = i - SKEW * row
        kd = i - SKEW * (last - row)

        @pl.when(jnp.logical_and(ku >= 0, ku < pieces))
        def _():
            own = jnp.where(from_home, home[ku], away[ku])

            @pl.when(row == 0)
            def _():
                up[ku] = own

            @pl.when(row > 0)
            def _():
                send_up(ku).wait_recv()
                up[ku] = jnp.where(here, own, up[ku])

            @pl.when(row < last)
            def _():
                send_up(ku).start()

        @pl.when(jnp.logical_and(kd >= 0, kd < pieces))
        def _():
            own = jnp.where(from_home, home[kd], away[kd])

            @pl.when(row == last)
            def _():
                down[kd] = own

            @pl.when(row < last)
            def _():
                send_down(kd).wait_recv()
                down[kd] = jnp.where(here, own, down[kd])

            @pl.when(row > 0)
            def _():
                send_down(kd).start()

        done = i - SKEW * depth

        @pl.when(jnp.logical_and(done >= 0, done < pieces))
        def _():
            mat[done] = jnp.where(below_or_here, up[done], down[done])

    load_at = X_HUB[-1] + Y_LAG + LOAD_LAG

    def arrive(n):
        group(partner, n, vec, x_send, x_sem.at[n], across).wait_recv()
        group(partner, n, vec, y_send, y_sem.at[n], over).start()
        group(partner, n, vec, d_send, d_sem, mate).start()

    def pass_on(n):
        group(partner, n, far_vec, y_send, y_sem.at[n], over).wait_recv()
        group(partner, n, far_vec, r_send, r_sem, mate).start()

    def load_partner():
        quarter_of(partner, d_send, d_sem).wait_recv()
        quarter_of(partner, r_send, r_sem).wait_recv()
        for w in range(per_dev):
            load(per_dev + w).start()

    def loaded(first):
        for w in range(per_dev):
            load(first + w).wait()

    def z_arrive(n):
        group(beyond, n, vec, zy_send, z_sem.at[n], z_to).wait_recv()
        group(beyond, n, vec, zy_send, zy_sem.at[n], over).start()
        group(beyond, n, vec, zd_send, zd_sem, mate).start()

    def z_pass_on(n):
        group(beyond, n, far_vec, zy_send, zy_sem.at[n], over).wait_recv()
        group(beyond, n, far_vec, zr_send, zr_sem, mate).start()

    half = DEEP // 2
    wide = half * LANES

    def multiply(b, w):
        p = state[w, pl.ds(pl.multiple_of(b * wide, wide), wide), :]
        re = jnp.concatenate([mat[b * DEEP + j] for j in range(half)], axis=1)
        im = jnp.concatenate([mat[b * DEEP + half + j] for j in range(half)], axis=1)
        x = jnp.dot(re, p, preferred_element_type=jnp.float32)
        y = jnp.dot(im, p, preferred_element_type=jnp.float32)
        acc[w, :, :electrons] += x[:, :electrons] - y[:, electrons:]
        acc[w, :, electrons:] += x[:, electrons:] + y[:, :electrons]

    def products(i):
        e = i - SKEW * depth - (DEEP - 1)
        def own_count(e, w):
            return clip(lax.div(e + DEEP - w, DEEP), 0, blocks)

        def partner_count(i, w):
            e = i - SKEW * depth - (DEEP - 1)
            full = clip(lax.div(e + DEEP, DEEP), 0, blocks)
            return jnp.where(i > total, blocks, clip((i - load_at - 2) * CATCH_UP, 0, full))

        spans = [(own_count(e - 1, w), own_count(e, w)) for w in range(per_dev)]
        spans += [(partner_count(i - 1, w), partner_count(i, w)) for w in range(per_dev)]
        def some(w, carry):
            lo, hi = spans[-1]
            for v in range(len(spans) - 1):
                lo = jnp.where(w == v, spans[v][0], lo)
                hi = jnp.where(w == v, spans[v][1], hi)
            lax.fori_loop(lo, hi, lambda b, c: (multiply(b, w), c)[1], 0)
            return carry
        lax.fori_loop(0, len(spans), some, 0)

    sub = lax.broadcasted_iota(jnp.int32, result.shape, 0)
    lane = lax.broadcasted_iota(jnp.int32, result.shape, 1)
    result[...] = jnp.zeros_like(result)
    orbitals = blocks * wide

    def finish(w):
        o = state[w, orbitals:, :]
        m = acc[w].astype(jnp.bfloat16)
        u = jnp.dot(m[:, :electrons], o, preferred_element_type=jnp.float32)
        v = jnp.dot(m[:, electrons:], o, preferred_element_type=jnp.float32)
        g_re = u[:, :electrons] - v[:, electrons:]
        g_im = u[:, electrons:] + v[:, :electrons]
        t_re, t_im = g_re.T, g_im.T
        eye = (lax.broadcasted_iota(jnp.int32, g_re.shape, 0)
               == lax.broadcasted_iota(jnp.int32, g_re.shape, 1))
        values = [
            jnp.sum(jnp.where(eye, g_re, 0.0)),
            jnp.sum(jnp.where(eye, g_im, 0.0)),
            jnp.sum(g_re * t_re - g_im * t_im),
            2.0 * jnp.sum(g_re * t_im),
        ]
        for n, value in enumerate(values):
            result[...] = jnp.where(jnp.logical_and(sub == w, lane == n), value, result[...])

    def tell(n):
        target, where = readers[n]
        return remote(result, table.at[where], t_send, t_sem, target)

    keep = pltpu.make_async_copy(result, table.at[place], keep_sem)

    def tell_all():
        for n in range(len(readers)):
            tell(n).start()
        keep.start()

    def hub_units():
        each(0, units, lambda u: x_unit(u).start())

    events, rest = [], []
    events.append((HUB_START, hub, functools.partial(hub_units)))
    for times, z_times, role in ((X_HUB, Z_HUB, hub), (X_LEAF, Z_LEAF, leaf)):
        late = []
        for n, end in enumerate(ends):
            at = times[min(n, len(times) - 1)]
            events.append((at, role, functools.partial(arrive, n)))
            events.append((at + Y_LAG, role, functools.partial(pass_on, n)))
            fewest = min(DIRECT[0], DIRECT_WRAP)
            span = z_times[1] - z_times[0]
            at = z_times[0] + -(-max(end - fewest, 0) * span // (units - fewest)) + Z_LAG
            if groups[n][0] < max(DIRECT[2], DIRECT_WRAP):
                at = max(at, RELAY + RELAY_LAG)
            for run, when in ((z_arrive, at), (z_pass_on, at + Z_LAG_Y)):
                if when < min(total, NEAR):
                    events.append((when, role, functools.partial(run, n)))
                else:
                    late.append((run, n))
        late.sort(key=lambda item: item[1] + (1 if item[0] is z_pass_on else 0))
        rest.append((role, late))
    events.append((RELAY, None, functools.partial(relay_all)))
    events.append((load_at, None, functools.partial(load_partner)))
    events.append((load_at + 2, None, functools.partial(loaded, per_dev)))
    events.append((min(DEEP - 1 + SKEW * (rows // 2), total), None, functools.partial(loaded, 0)))

    def handle(start, stop):
        for role, late in rest:
            @pl.when(role)
            def _():
                for run, n in late[start:stop]:
                    run(n)

    after = [
        lambda: each(sent(total - 1), units, lambda u: z_unit(u).start()),
        functools.partial(handle, 0, 1),
        lambda: each(total, total + 2, products),
    ]
    for w in range(2 * per_dev):
        after.append(functools.partial(handle, w + 1, w + 2))
        after.append(functools.partial(finish, w))
    after.append(tell_all)
    after.append(functools.partial(handle, 2 * per_dev + 1, 10 * len(groups)))

    families = {}
    for when, role, run in events:
        families.setdefault((run.func, when // SPAN) if role is not None else None, []).append((when, role, run))

    def step(i):
        chain(i)
        for members in families.values():
            times = [when for when, _, _ in members]

            @pl.when(jnp.logical_and(i >= min(times), i <= max(times)))
            def _():
                for when, role, run in members:
                    pl.when(i == when if role is None else jnp.logical_and(i == when, role))(run)
        each(jnp.where(i == 0, direct_sent(0), direct_sent(i - 1)), direct_sent(i), lambda u: direct_unit(u).start())
        each(sent(i - 1), sent(i), lambda u: z_unit(u).start())
        products(i)

    each(0, total, step)
    for run in after:
        run()


    quarter_of(beyond, zd_send, zd_sem).wait_recv()
    quarter_of(beyond, zr_send, zr_sem).wait_recv()

    def all_sent(buffer, send, target):
        remote(buffer, buffer, send, t_sem, target).wait_send()

    @pl.when(hub)
    def _():
        send_note.wait_send()
        all_sent(home, mate_send, mate)
        all_sent(away, relay_send, mate)

    @pl.when(leaf)
    def _():
        all_sent(away, across_send, across)

    @pl.when(row < last)
    def _():
        all_sent(up, up_send, above)

    @pl.when(row > 0)
    def _():
        all_sent(down, down_send, below)

    part = partner.at[:, pl.ds(pl.multiple_of(vec * quarter, UNIT), quarter)]
    for send, target in (
        (x_send, across), (y_send, over), (d_send, mate), (r_send, mate),
        (zy_send, over), (zd_send, mate), (zr_send, mate),
    ):
        all_sent(part, send, target)

    keep.wait()
    for count in range(min(DIRECT[0], DIRECT_WRAP), max(DIRECT[2], DIRECT_WRAP) + 1):
        @pl.when(skip == count)
        def _():
            some = partner.at[:, pl.ds(0, (units - count) * UNIT)]
            all_sent(some, z_send, z_to)

    each(0, direct_count(order_own), lambda u: direct_unit(u).wait_send())
    each(0, direct_count(lax.rem(order_own + last, rows)), lambda u: relay_unit(u).wait_send())

    heard = table.at[pl.ds(0, len(readers))]
    remote(heard, heard, t_send, t_sem, mate).wait_send()

    remote(heard, heard, t_send, t_sem, mate).wait_recv()


def step_all(n_walk, n_vec, owners, chol, walkers):
    per_dev, height, width = walkers.shape
    electrons, orbitals = chol.shape[2:]
    pieces = orbitals // LANES
    units = height // n_vec // UNIT
    groups = -(-units // GROUP)
    most = max(DIRECT[2], DIRECT_WRAP)
    big = pltpu.VMEM((pieces, electrons, LANES), chol.dtype)
    dma = pltpu.SemaphoreType.DMA
    any_spec = pl.BlockSpec(memory_space=pl.ANY)
    smem = pl.BlockSpec(memory_space=pltpu.SMEM)
    same = jax.ShapeDtypeStruct(walkers.shape, walkers.dtype)
    return pl.pallas_call(
        functools.partial(step_kernel, n_walk, n_vec),
        out_shape=(jax.ShapeDtypeStruct((4 * n_vec, 8, 128), jnp.float32), same, same),
        in_specs=[smem, any_spec, any_spec],
        out_specs=(any_spec, any_spec, any_spec),
        scratch_shapes=[
            big, big, big, big, big,
            pltpu.VMEM((max(DIRECT[2], DIRECT_WRAP), per_dev, UNIT, width), walkers.dtype),
            pltpu.VMEM((2 * per_dev, height, width), walkers.dtype),
            pltpu.VMEM((2 * per_dev, electrons, width), jnp.float32),
            pltpu.VMEM((8, 128), jnp.float32),
            pltpu.VMEM((8, 128), jnp.float32),
            pltpu.VMEM((8, 128), jnp.float32),
        ] + [dma((-(-pieces // BATCH),))] + [dma((pieces,))] * 3 + [dma] * 12 + [dma] + [dma((most,))] * 3 + [dma((groups,))] * 4 + [dma] * 4
        + [dma((2 * per_dev,)), dma, dma, dma, dma, dma],
        compiler_params=pltpu.CompilerParams(
            collective_id=0, has_side_effects=True, vmem_limit_bytes=62 * 1024 * 1024),
        name="step_all",
    )(owners, chol, walkers)


BITS = 4


def branch_kernel(
    n_walk, n_vec, slots, walkers, partner, beyond, table,
    branched, bias, energy, held, facts, in_sem, out_sem, t_sem,
):
    walk, vec = lax.axis_index("walk"), lax.axis_index("vec")
    col = lax.rem(walk, 2)
    per_dev, height = walkers.shape[:2]
    piece = height // BITS
    total = per_dev * n_walk

    def rows(t):
        return pl.ds(t * piece, piece)

    def fetch(buffer, w, s, t):
        return pltpu.make_async_copy(buffer.at[w, rows(t)], held.at[s, rows(t)], in_sem.at[s, t])

    def put(s, t):
        return pltpu.make_async_copy(held.at[s, rows(t)], branched.at[s, rows(t)], out_sem.at[s, t])

    cases = [(s, t) for s in range(per_dev) for t in range(BITS)]
    picks = []
    for s in range(per_dev):
        relative = lax.rem(slots[s] - (walk - 1) * per_dev + total, total)
        side, w = lax.div(relative, per_dev), lax.rem(relative, per_dev)
        mine, beside = side == 1, side == 2 * (1 - col)
        far = jnp.logical_not(jnp.logical_or(mine, beside))
        picks.append((w, jnp.where(far, 1, 0), jnp.where(mine, col, 1 - col)))
        for wanted, buffer in ((mine, walkers), (beside, partner), (far, beyond)):
            @pl.when(wanted)
            def _():
                for t in range(BITS):
                    fetch(buffer, w, s, t).start()
    facts_in = pltpu.make_async_copy(table, facts, t_sem)
    facts_in.start()
    for s, t in cases:
        fetch(walkers, 0, s, t).wait()
        put(s, t).start()
    facts_in.wait()

    for s, (w, far, block) in enumerate(picks):
        def value(v, g, lane):
            sender = lax.rem(v, 2)
            at = far * 2 * n_vec + sender * n_vec + lax.div(v, 2) * 2 + g
            return facts[at, jnp.where(block == sender, 0, per_dev) + w, lane]

        for g in range(2):
            for part in range(2):
                bias[s, g, part] = value(vec, g, part)
        for part in range(2):
            energy[s, part] = -0.5 * sum(value(jnp.int32(v), g, 2 + part) for v in range(n_vec) for g in range(2))

    for s, t in cases:
        put(s, t).wait()


def branch(n_walk, n_vec, slots, walkers, partner, beyond, table):
    per_dev = walkers.shape[0]
    dma = pltpu.SemaphoreType.DMA
    any_spec = pl.BlockSpec(memory_space=pl.ANY)
    smem = pl.BlockSpec(memory_space=pltpu.SMEM)
    return pl.pallas_call(
        functools.partial(branch_kernel, n_walk, n_vec),
        out_shape=(
            jax.ShapeDtypeStruct(walkers.shape, walkers.dtype),
            jax.ShapeDtypeStruct((per_dev, 2, 2), jnp.float32),
            jax.ShapeDtypeStruct((per_dev, 2), jnp.float32),
        ),
        in_specs=[smem, any_spec, any_spec, any_spec, any_spec],
        out_specs=(any_spec, smem, smem),
        scratch_shapes=[
            pltpu.VMEM(walkers.shape, walkers.dtype), pltpu.SMEM(table.shape, table.dtype),
            dma((per_dev, BITS)), dma((per_dev, BITS)), dma,
        ],
        compiler_params=pltpu.CompilerParams(vmem_limit_bytes=62 * 1024 * 1024),
        name="branch",
    )(slots, walkers, partner, beyond, table)


def shards(n_walk, n_vec, walkers, chol, owners, branch_src):
    table, partner, beyond = step_all(n_walk, n_vec, owners, chol, walkers)
    return branch(n_walk, n_vec, branch_src, walkers, partner, beyond, table)


def solution(mesh):
    n_walk, n_vec = mesh.shape["walk"], mesh.shape["vec"]
    return jax.shard_map(
        functools.partial(shards, n_walk, n_vec),
        mesh=mesh,
        in_specs=(P("walk", None, None), P("vec", "walk", None, None), P("vec", None), P("walk")),
        out_specs=(P("walk", None, None), P("walk", "vec", None), P("walk", None)),
        check_vma=False,
    )
```

```python
import functools

import jax
import jax.numpy as jnp
from jax import lax
from jax.experimental import pallas as pl
from jax.experimental.pallas import tpu as pltpu
from jax.sharding import PartitionSpec as P

MESH = pl.DeviceIdType.MESH
LANES = 128
DEEP = 4
UNIT = 32
GROUP = 2
SKEW = 3
AHEAD = 8
BATCH = 4
RING = 16
X_SLOW = (17, 100)
X_FAST = 2
X_HUB = (16, 17, 18, 19, 20, 21, 23, 24, 25, 25)
X_LEAF = (4, 6, 8, 9, 11, 12, 13, 15, 16, 17)
Y_LAG = 3
LOAD_LAG = 2
CATCH_UP = 1
Z_HUB = (16, 33)
Z_LEAF = (6, 33)
HUB_START = 0
Z_LAG = 4
Z_LAG_Y = 3
NEAR = 41
RELAY = 22
RELAY_LAG = 5
DIRECT = (2, 1, 4)
DIRECT_WRAP = 3
WRAP_START = 4
WRAP_STEPS = 2
SPAN = 8


def flip(index):
    return index + 1 - 2 * lax.rem(index, 2)


def clip(value, low, high):
    return jnp.minimum(jnp.maximum(value, low), high)


def step_kernel(
    n_walk, n_vec, owners, chol, walkers, table, partner, beyond,
    home, away, up, down, mat, hold, state, acc, result, note, told,
    home_sem, away_sem, up_sem, down_sem,
    mate_send, across_send, relay_send, up_send, down_send,
    x_send, y_send, d_send, r_send, zy_send, zd_send, zr_send, z_send, direct_send, hold_send, hold_sem,
    x_sem, y_sem, z_sem, zy_sem, d_sem, r_sem, zd_sem, zr_sem,
    load_sem, keep_sem, note_send, note_sem, t_send, t_sem,
):
    walk, vec = lax.axis_index("walk"), lax.axis_index("vec")
    rows = n_walk // 2
    last = rows - 1
    row, col = walk // 2, lax.rem(walk, 2)
    low = lax.rem(vec, 2)
    hub = low == col
    leaf = jnp.logical_not(hub)
    pieces, electrons = home.shape[0], home.shape[1]
    blocks = pieces // DEEP
    per_dev = walkers.shape[0]
    quarter = walkers.shape[1] // n_vec
    units = quarter // UNIT
    groups = [(first, min(GROUP, units - first)) for first in range(0, units, GROUP)]
    ends = [first + size for first, size in groups]
    flip_walk, flip_vec = flip(walk), flip(vec)
    far_vec = lax.rem(vec + 2, n_vec)
    z_next = lax.rem(row + 1 - 2 * col + rows, rows)
    order = jnp.where(col == 0, row, last - row)
    order_own = last - order
    z_own = lax.rem(row + 2 * col - 1 + rows, rows)
    direct_to = {"walk": z_own * 2 + col, "vec": vec}
    z_to = {"walk": z_next * 2 + col, "vec": vec}
    across = {"walk": flip_walk, "vec": vec}
    mate = {"walk": walk, "vec": flip_vec}
    over = {"walk": walk, "vec": far_vec}
    above = {"walk": walk + 2, "vec": vec}
    below = {"walk": walk - 2, "vec": vec}
    row_up, row_down = lax.rem(row + 1, rows), lax.rem(row + rows - 1, rows)

    place = col * n_vec + vec
    readers = [({"walk": walk, "vec": lax.rem(vec + j, n_vec)}, place) for j in range(1, n_vec)]
    readers += [({"walk": flip_walk, "vec": lax.rem(vec + j, n_vec)}, place) for j in range(n_vec)]
    readers += [({"walk": row_up * 2, "vec": lax.rem(vec + j, n_vec)}, place + 2 * n_vec) for j in range(n_vec)]
    readers += [({"walk": row_down * 2 + 1, "vec": lax.rem(vec + j, n_vec)}, place + 2 * n_vec) for j in range(n_vec)]

    def each(lo, hi, f):
        def body(k, carry):
            f(k)
            return carry
        lax.fori_loop(lo, hi, body, 0)

    def remote(src, dst, send, recv, target):
        return pltpu.make_async_remote_copy(
            src_ref=src, dst_ref=dst, send_sem=send, recv_sem=recv,
            device_id=target, device_id_type=MESH)

    def chol_piece(k):
        b, j = lax.div(k, DEEP), lax.rem(k, DEEP)
        half = DEEP // 2
        at = b * half + jnp.where(j < half, j, j - half + blocks * half)
        return chol.at[0, 0, :, pl.ds(pl.multiple_of(at * LANES, LANES), LANES)]

    def own_to_home(k):
        return pltpu.make_async_copy(chol_piece(k), home.at[k], home_sem.at[lax.div(k, BATCH)])

    def home_batch(k):
        return home.at[pl.ds(k, BATCH)]

    def own_to_mate(k):
        return remote(chol_piece(k), home.at[k], mate_send, home_sem.at[lax.div(k, BATCH)], mate)

    def own_across(k):
        return remote(chol_piece(k), away.at[k], across_send, away_sem.at[k], across)

    def away_to_mate(k):
        return remote(away.at[k], away.at[k], relay_send, away_sem.at[k], mate)

    def send_up(k):
        return remote(up.at[k], up.at[k], up_send, up_sem.at[lax.rem(k, up_sem.shape[0])], above)

    def send_down(k):
        return remote(down.at[k], down.at[k], down_send, down_sem.at[lax.rem(k, down_sem.shape[0])], below)

    def unit_rows(u):
        return pl.ds(pl.multiple_of(vec * quarter + u * UNIT, UNIT), UNIT)

    def x_unit(u):
        at = unit_rows(u)
        return remote(walkers.at[:, at], partner.at[:, at], x_send, x_sem.at[lax.div(u, GROUP)], across)

    def z_unit(u):
        at = unit_rows(u)
        return remote(partner.at[:, at], beyond.at[:, at], z_send, z_sem.at[lax.div(u, GROUP)], z_to)

    def direct_unit(u):
        at = unit_rows(u)
        return remote(walkers.at[:, at], hold.at[u], direct_send.at[u], hold_sem.at[u], direct_to)

    def relay_unit(u):
        at = unit_rows(u)
        return remote(hold.at[u], beyond.at[:, at], hold_send.at[u], z_sem.at[lax.div(u, GROUP)], across)

    def direct_count(position):
        return jnp.where(position == last, DIRECT_WRAP,
                         jnp.minimum(DIRECT[0] + DIRECT[1] * position, DIRECT[2]))

    def relay_all():
        def one(u):
            direct_unit(u).wait_recv()
            relay_unit(u).start()
        each(0, direct_count(lax.rem(order_own + last, rows)), one)

    def direct_sent(i):
        paced = clip(lax.div(i - WRAP_START + WRAP_STEPS, WRAP_STEPS), 0, DIRECT_WRAP)
        return jnp.where(order_own == last, paced, direct_count(order_own))

    def group(buffer, n, index, send, recv, target):
        first, size = groups[n]
        at = pl.ds(pl.multiple_of(index * quarter + first * UNIT, UNIT), size * UNIT)
        return remote(buffer.at[:, at], buffer.at[:, at], send, recv, target)

    def quarter_of(buffer, send, recv):
        at = pl.ds(pl.multiple_of(vec * quarter, UNIT), quarter)
        return remote(buffer.at[:, at], buffer.at[:, at], send, recv, mate)

    def load(w):
        src = walkers.at[w] if w < per_dev else partner.at[w - per_dev]
        return pltpu.make_async_copy(src, state.at[w], load_sem.at[w])

    bar = pltpu.get_barrier_semaphore()
    for target in (
        [t for t, _ in readers[:2 * n_vec - 1]]
        + [{"walk": r * 2 + c, "vec": lax.rem(vec + j, n_vec)}
           for r in (row_up, row_down) for c in range(2) for j in range(n_vec)]
    ):
        pl.semaphore_signal(bar, inc=1, device_id=target, device_id_type=MESH)
    for w in range(per_dev):
        load(w).start()

    @pl.when(hub)
    def _():
        each(0, pieces, lambda k: own_to_home(k).start())

    def code_of(root):
        here = (lax.div(root, 2) == row).astype(jnp.float32)
        under = (lax.div(root, 2) <= row).astype(jnp.float32)
        at_home = (lax.rem(root, 2) == col).astype(jnp.float32)
        return here + 2.0 * under + 4.0 * at_home

    code_mate = jnp.where(low == 0, code_of(owners[0, 1]), code_of(owners[0, 0]))
    code_own = jnp.where(low == 0, code_of(owners[0, 0]), code_of(owners[0, 1]))
    note[...] = jnp.full(note.shape, code_mate, jnp.float32)

    @pl.when(hub)
    def _():
        told[...] = jnp.full(told.shape, code_own, jnp.float32)

    send_note = remote(note, told, note_send, note_sem, mate)

    pl.semaphore_wait(bar, 6 * n_vec - 1)

    each(0, direct_sent(0), lambda u: direct_unit(u).start())

    @pl.when(hub)
    def _():
        send_note.start()
        each(0, min(AHEAD, pieces), lambda k: own_to_mate(k).start())

    @pl.when(leaf)
    def _():
        def x_count(k):
            slow = lax.div(jnp.minimum(k, X_SLOW[0]), X_SLOW[1])
            return jnp.minimum(slow + jnp.maximum(k - X_SLOW[0], 0) * X_FAST, units)

        def start(k):
            own_across(k).start()
            each(x_count(k), x_count(k + 1), lambda u: x_unit(u).start())
        each(0, pieces, start)
        each(x_count(pieces), units, lambda u: x_unit(u).start())

    acc[...] = jnp.zeros_like(acc)

    @pl.when(leaf)
    def _():
        send_note.wait_recv()

    code = jnp.max(told[...])
    from_home = code >= 4.0
    code = jnp.where(from_home, code - 4.0, code)
    below_or_here = code >= 2.0
    here = jnp.where(below_or_here, code - 2.0, code) >= 1.0
    total = pieces + SKEW * last
    depth = jnp.maximum(row, last - row)

    skip = direct_count(order)

    def sent(i):
        gone = jnp.where(
            hub,
            lax.div(jnp.maximum(i - Z_HUB[0], 0) * (units - skip), Z_HUB[1] - Z_HUB[0]),
            lax.div(jnp.maximum(i - Z_LEAF[0], 0) * (units - skip), Z_LEAF[1] - Z_LEAF[0]))
        return jnp.minimum(skip + gone, units)

    def chain(i):
        @pl.when(i < pieces)
        def _():
            @pl.when(hub)
            def _():
                own_across(i).wait_recv()
                away_to_mate(i).start()

                @pl.when(i + AHEAD < pieces)
                def _():
                    own_to_mate(i + AHEAD).start()

                @pl.when(lax.rem(i, BATCH) == 0)
                def _():
                    pltpu.make_async_copy(home_batch(i), home_batch(i), home_sem.at[lax.div(i, BATCH)]).wait()

            @pl.when(leaf)
            def _():
                @pl.when(lax.rem(i, BATCH) == 0)
                def _():
                    remote(home_batch(i), home_batch(i), mate_send, home_sem.at[lax.div(i, BATCH)], mate).wait_recv()

                away_to_mate(i).wait_recv()

        ku = i - SKEW * row
        kd = i - SKEW * (last - row)

        @pl.when(jnp.logical_and(ku >= 0, ku < pieces))
        def _():
            own = jnp.where(from_home, home[ku], away[ku])

            @pl.when(row == 0)
            def _():
                up[ku] = own

            @pl.when(row > 0)
            def _():
                send_up(ku).wait_recv()
                up[ku] = jnp.where(here, own, up[ku])

            @pl.when(row < last)
            def _():
                send_up(ku).start()

        @pl.when(jnp.logical_and(kd >= 0, kd < pieces))
        def _():
            own = jnp.where(from_home, home[kd], away[kd])

            @pl.when(row == last)
            def _():
                down[kd] = own

            @pl.when(row < last)
            def _():
                send_down(kd).wait_recv()
                down[kd] = jnp.where(here, own, down[kd])

            @pl.when(row > 0)
            def _():
                send_down(kd).start()

        done = i - SKEW * depth

        @pl.when(jnp.logical_and(done >= 0, done < pieces))
        def _():
            mat[done] = jnp.where(below_or_here, up[done], down[done])

    load_at = X_HUB[-1] + Y_LAG + LOAD_LAG

    def arrive(n):
        group(partner, n, vec, x_send, x_sem.at[n], across).wait_recv()
        group(partner, n, vec, y_send, y_sem.at[n], over).start()
        group(partner, n, vec, d_send, d_sem, mate).start()

    def pass_on(n):
        group(partner, n, far_vec, y_send, y_sem.at[n], over).wait_recv()
        group(partner, n, far_vec, r_send, r_sem, mate).start()

    def load_partner():
        quarter_of(partner, d_send, d_sem).wait_recv()
        quarter_of(partner, r_send, r_sem).wait_recv()
        for w in range(per_dev):
            load(per_dev + w).start()

    def loaded(first):
        for w in range(per_dev):
            load(first + w).wait()

    def z_arrive(n):
        group(beyond, n, vec, zy_send, z_sem.at[n], z_to).wait_recv()
        group(beyond, n, vec, zy_send, zy_sem.at[n], over).start()
        group(beyond, n, vec, zd_send, zd_sem, mate).start()

    def z_pass_on(n):
        group(beyond, n, far_vec, zy_send, zy_sem.at[n], over).wait_recv()
        group(beyond, n, far_vec, zr_send, zr_sem, mate).start()

    half = DEEP // 2
    wide = half * LANES

    def multiply(b, w):
        p = state[w, pl.ds(pl.multiple_of(b * wide, wide), wide), :]
        re = jnp.concatenate([mat[b * DEEP + j] for j in range(half)], axis=1)
        im = jnp.concatenate([mat[b * DEEP + half + j] for j in range(half)], axis=1)
        x = jnp.dot(re, p, preferred_element_type=jnp.float32)
        y = jnp.dot(im, p, preferred_element_type=jnp.float32)
        acc[w, :, :electrons] += x[:, :electrons] - y[:, electrons:]
        acc[w, :, electrons:] += x[:, electrons:] + y[:, :electrons]

    def products(i):
        e = i - SKEW * depth - (DEEP - 1)
        def own_count(e, w):
            return clip(lax.div(e + DEEP - w, DEEP), 0, blocks)

        def partner_count(i, w):
            e = i - SKEW * depth - (DEEP - 1)
            full = clip(lax.div(e + DEEP, DEEP), 0, blocks)
            return jnp.where(i > total, blocks, clip((i - load_at - 2) * CATCH_UP, 0, full))

        spans = [(own_count(e - 1, w), own_count(e, w)) for w in range(per_dev)]
        spans += [(partner_count(i - 1, w), partner_count(i, w)) for w in range(per_dev)]
        def some(w, carry):
            lo, hi = spans[-1]
            for v in range(len(spans) - 1):
                lo = jnp.where(w == v, spans[v][0], lo)
                hi = jnp.where(w == v, spans[v][1], hi)
            lax.fori_loop(lo, hi, lambda b, c: (multiply(b, w), c)[1], 0)
            return carry
        lax.fori_loop(0, len(spans), some, 0)

    sub = lax.broadcasted_iota(jnp.int32, result.shape, 0)
    lane = lax.broadcasted_iota(jnp.int32, result.shape, 1)
    result[...] = jnp.zeros_like(result)
    orbitals = blocks * wide

    def finish(w):
        o = state[w, orbitals:, :]
        m = acc[w].astype(jnp.bfloat16)
        u = jnp.dot(m[:, :electrons], o, preferred_element_type=jnp.float32)
        v = jnp.dot(m[:, electrons:], o, preferred_element_type=jnp.float32)
        g_re = u[:, :electrons] - v[:, electrons:]
        g_im = u[:, electrons:] + v[:, :electrons]
        side = LANES if electrons % LANES == 0 else electrons
        eye = (lax.broadcasted_iota(jnp.int32, (side, side), 0)
               == lax.broadcasted_iota(jnp.int32, (side, side), 1))
        spots = range(0, electrons, side)

        def tile(g, a, b):
            return g[a:a + side, b:b + side]

        ex_re = ex_im = bias_re = bias_im = jnp.zeros((side, side), jnp.float32)
        for a in spots:
            bias_re = bias_re + tile(g_re, a, a)
            bias_im = bias_im + tile(g_im, a, a)
            for b in spots:
                if b < a:
                    continue
                times = 1.0 if a == b else 2.0
                re, im = tile(g_re, a, b), tile(g_im, a, b)
                t_re, t_im = tile(g_re, b, a).T, tile(g_im, b, a).T
                ex_re = ex_re + times * (re * t_re - im * t_im)
                ex_im = ex_im + times * (re * t_im + im * t_re)
        values = [
            jnp.sum(jnp.where(eye, bias_re, 0.0)),
            jnp.sum(jnp.where(eye, bias_im, 0.0)),
            jnp.sum(ex_re),
            jnp.sum(ex_im),
        ]
        for n, value in enumerate(values):
            result[...] = jnp.where(jnp.logical_and(sub == w, lane == n), value, result[...])

    def tell(n):
        target, where = readers[n]
        return remote(result, table.at[where], t_send, t_sem, target)

    keep = pltpu.make_async_copy(result, table.at[place], keep_sem)

    def tell_all():
        for n in range(len(readers)):
            tell(n).start()
        keep.start()

    def hub_units():
        each(0, units, lambda u: x_unit(u).start())

    events, rest = [], []
    events.append((HUB_START, hub, functools.partial(hub_units)))
    for times, z_times, role in ((X_HUB, Z_HUB, hub), (X_LEAF, Z_LEAF, leaf)):
        late = []
        for n, end in enumerate(ends):
            at = times[min(n, len(times) - 1)]
            events.append((at, role, functools.partial(arrive, n)))
            events.append((at + Y_LAG, role, functools.partial(pass_on, n)))
            fewest = min(DIRECT[0], DIRECT_WRAP)
            span = z_times[1] - z_times[0]
            at = z_times[0] + -(-max(end - fewest, 0) * span // (units - fewest)) + Z_LAG
            if groups[n][0] < max(DIRECT[2], DIRECT_WRAP):
                at = max(at, RELAY + RELAY_LAG)
            for run, when in ((z_arrive, at), (z_pass_on, at + Z_LAG_Y)):
                if when < min(total, NEAR):
                    events.append((when, role, functools.partial(run, n)))
                else:
                    late.append((run, n))
        late.sort(key=lambda item: item[1] + (1 if item[0] is z_pass_on else 0))
        rest.append((role, late))
    events.append((RELAY, None, functools.partial(relay_all)))
    events.append((load_at, None, functools.partial(load_partner)))
    events.append((load_at + 2, None, functools.partial(loaded, per_dev)))
    events.append((min(DEEP - 1 + SKEW * (rows // 2), total), None, functools.partial(loaded, 0)))

    def handle(start, stop):
        for role, late in rest:
            @pl.when(role)
            def _():
                for run, n in late[start:stop]:
                    run(n)

    after = [
        lambda: each(sent(total - 1), units, lambda u: z_unit(u).start()),
        functools.partial(handle, 0, 1),
        lambda: each(total, total + 2, products),
    ]
    for w in range(2 * per_dev):
        after.append(functools.partial(handle, w + 1, w + 2))
        after.append(functools.partial(finish, w))
    after.append(tell_all)
    after.append(functools.partial(handle, 2 * per_dev + 1, 10 * len(groups)))

    families = {}
    for when, role, run in events:
        families.setdefault((run.func, when // SPAN) if role is not None else None, []).append((when, role, run))

    def step(i):
        chain(i)
        for members in families.values():
            times = [when for when, _, _ in members]

            @pl.when(jnp.logical_and(i >= min(times), i <= max(times)))
            def _():
                for when, role, run in members:
                    pl.when(i == when if role is None else jnp.logical_and(i == when, role))(run)
        each(jnp.where(i == 0, direct_sent(0), direct_sent(i - 1)), direct_sent(i), lambda u: direct_unit(u).start())
        each(sent(i - 1), sent(i), lambda u: z_unit(u).start())
        products(i)

    each(0, total, step)
    for run in after:
        run()


    quarter_of(beyond, zd_send, zd_sem).wait_recv()
    quarter_of(beyond, zr_send, zr_sem).wait_recv()

    def all_sent(buffer, send, target):
        remote(buffer, buffer, send, t_sem, target).wait_send()

    @pl.when(hub)
    def _():
        send_note.wait_send()
        all_sent(home, mate_send, mate)
        all_sent(away, relay_send, mate)

    @pl.when(leaf)
    def _():
        all_sent(away, across_send, across)

    @pl.when(row < last)
    def _():
        all_sent(up, up_send, above)

    @pl.when(row > 0)
    def _():
        all_sent(down, down_send, below)

    part = partner.at[:, pl.ds(pl.multiple_of(vec * quarter, UNIT), quarter)]
    for send, target in (
        (x_send, across), (y_send, over), (d_send, mate), (r_send, mate),
        (zy_send, over), (zd_send, mate), (zr_send, mate),
    ):
        all_sent(part, send, target)

    keep.wait()
    for count in range(min(DIRECT[0], DIRECT_WRAP), max(DIRECT[2], DIRECT_WRAP) + 1):
        @pl.when(skip == count)
        def _():
            some = partner.at[:, pl.ds(0, (units - count) * UNIT)]
            all_sent(some, z_send, z_to)

    each(0, direct_count(order_own), lambda u: direct_unit(u).wait_send())
    each(0, direct_count(lax.rem(order_own + last, rows)), lambda u: relay_unit(u).wait_send())

    heard = table.at[pl.ds(0, len(readers))]
    remote(heard, heard, t_send, t_sem, mate).wait_send()

    remote(heard, heard, t_send, t_sem, mate).wait_recv()


def step_all(n_walk, n_vec, owners, chol, walkers):
    per_dev, height, width = walkers.shape
    electrons, orbitals = chol.shape[2:]
    pieces = orbitals // LANES
    units = height // n_vec // UNIT
    groups = -(-units // GROUP)
    most = max(DIRECT[2], DIRECT_WRAP)
    ring = RING if SKEW * (n_walk // 2 - 1) < RING < pieces else pieces
    big = pltpu.VMEM((pieces, electrons, LANES), chol.dtype)
    dma = pltpu.SemaphoreType.DMA
    any_spec = pl.BlockSpec(memory_space=pl.ANY)
    smem = pl.BlockSpec(memory_space=pltpu.SMEM)
    same = jax.ShapeDtypeStruct(walkers.shape, walkers.dtype)
    return pl.pallas_call(
        functools.partial(step_kernel, n_walk, n_vec),
        out_shape=(jax.ShapeDtypeStruct((4 * n_vec, 8, 128), jnp.float32), same, same),
        in_specs=[smem, any_spec, any_spec],
        out_specs=(any_spec, any_spec, any_spec),
        scratch_shapes=[
            big, big, big, big, big,
            pltpu.VMEM((max(DIRECT[2], DIRECT_WRAP), per_dev, UNIT, width), walkers.dtype),
            pltpu.VMEM((2 * per_dev, height, width), walkers.dtype),
            pltpu.VMEM((2 * per_dev, electrons, width), jnp.float32),
            pltpu.VMEM((8, 128), jnp.float32),
            pltpu.VMEM((8, 128), jnp.float32),
            pltpu.VMEM((8, 128), jnp.float32),
        ] + [dma((-(-pieces // BATCH),))] + [dma((pieces,))] + [dma((ring,))] * 2 + [dma] * 12 + [dma] + [dma((most,))] * 3 + [dma((groups,))] * 4 + [dma] * 4
        + [dma((2 * per_dev,)), dma, dma, dma, dma, dma],
        compiler_params=pltpu.CompilerParams(
            collective_id=0, has_side_effects=True, vmem_limit_bytes=62 * 1024 * 1024),
        name="step_all",
    )(owners, chol, walkers)


BITS = 4


def branch_kernel(
    n_walk, n_vec, slots, walkers, partner, beyond, table,
    branched, bias, energy, held, facts, in_sem, out_sem, t_sem,
):
    walk, vec = lax.axis_index("walk"), lax.axis_index("vec")
    col = lax.rem(walk, 2)
    per_dev, height = walkers.shape[:2]
    piece = height // BITS
    total = per_dev * n_walk

    def rows(t):
        return pl.ds(t * piece, piece)

    def fetch(buffer, w, s, t):
        return pltpu.make_async_copy(buffer.at[w, rows(t)], held.at[s, rows(t)], in_sem.at[s, t])

    def put(s, t):
        return pltpu.make_async_copy(held.at[s, rows(t)], branched.at[s, rows(t)], out_sem.at[s, t])

    cases = [(s, t) for s in range(per_dev) for t in range(BITS)]
    picks = []
    for s in range(per_dev):
        relative = lax.rem(slots[s] - (walk - 1) * per_dev + total, total)
        side, w = lax.div(relative, per_dev), lax.rem(relative, per_dev)
        mine, beside = side == 1, side == 2 * (1 - col)
        far = jnp.logical_not(jnp.logical_or(mine, beside))
        picks.append((w, jnp.where(far, 1, 0), jnp.where(mine, col, 1 - col)))
        for wanted, buffer in ((mine, walkers), (beside, partner), (far, beyond)):
            @pl.when(wanted)
            def _():
                for t in range(BITS):
                    fetch(buffer, w, s, t).start()
    facts_in = pltpu.make_async_copy(table, facts, t_sem)
    facts_in.start()
    for s, t in cases:
        fetch(walkers, 0, s, t).wait()
        put(s, t).start()
    facts_in.wait()

    for s, (w, far, block) in enumerate(picks):
        def value(v, g, lane):
            sender = lax.rem(v, 2)
            at = far * 2 * n_vec + sender * n_vec + lax.div(v, 2) * 2 + g
            return facts[at, jnp.where(block == sender, 0, per_dev) + w, lane]

        for g in range(2):
            for part in range(2):
                bias[s, g, part] = value(vec, g, part)
        for part in range(2):
            energy[s, part] = -0.5 * sum(value(jnp.int32(v), g, 2 + part) for v in range(n_vec) for g in range(2))

    for s, t in cases:
        put(s, t).wait()


def branch(n_walk, n_vec, slots, walkers, partner, beyond, table):
    per_dev = walkers.shape[0]
    dma = pltpu.SemaphoreType.DMA
    any_spec = pl.BlockSpec(memory_space=pl.ANY)
    smem = pl.BlockSpec(memory_space=pltpu.SMEM)
    return pl.pallas_call(
        functools.partial(branch_kernel, n_walk, n_vec),
        out_shape=(
            jax.ShapeDtypeStruct(walkers.shape, walkers.dtype),
            jax.ShapeDtypeStruct((per_dev, 2, 2), jnp.float32),
            jax.ShapeDtypeStruct((per_dev, 2), jnp.float32),
        ),
        in_specs=[smem, any_spec, any_spec, any_spec, any_spec],
        out_specs=(any_spec, smem, smem),
        scratch_shapes=[
            pltpu.VMEM(walkers.shape, walkers.dtype), pltpu.SMEM(table.shape, table.dtype),
            dma((per_dev, BITS)), dma((per_dev, BITS)), dma,
        ],
        compiler_params=pltpu.CompilerParams(vmem_limit_bytes=62 * 1024 * 1024),
        name="branch",
    )(slots, walkers, partner, beyond, table)


def shards(n_walk, n_vec, walkers, chol, owners, branch_src):
    table, partner, beyond = step_all(n_walk, n_vec, owners, chol, walkers)
    return branch(n_walk, n_vec, branch_src, walkers, partner, beyond, table)


def solution(mesh):
    n_walk, n_vec = mesh.shape["walk"], mesh.shape["vec"]
    return jax.shard_map(
        functools.partial(shards, n_walk, n_vec),
        mesh=mesh,
        in_specs=(P("walk", None, None), P("vec", "walk", None, None), P("vec", None), P("walk")),
        out_specs=(P("walk", None, None), P("walk", "vec", None), P("walk", None)),
        check_vma=False,
    )
```

```python
import functools

import jax
import jax.numpy as jnp
from jax import lax
from jax.experimental import pallas as pl
from jax.experimental.pallas import tpu as pltpu
from jax.sharding import PartitionSpec as P

MESH = pl.DeviceIdType.MESH
LANES = 128
DEEP = 4
UNIT = 32
GROUP = 2
SKEW = 3
AHEAD = 8
BATCH = 4
RING = 16
X_SLOW = (16, 100)
X_FAST = 2
X_HUB = (16, 17, 18, 19, 20, 21, 23, 24, 25, 25)
X_LEAF = (6, 7, 9, 10, 12, 13, 14, 16, 17, 18)
Y_LAG = 3
LOAD_LAG = 2
CATCH_UP = 1
Z_HUB = (16, 33)
Z_LEAF = (8, 34)
HUB_START = 3
Z_LAG = 4
Z_LAG_Y = 3
NEAR = 41
RELAY = 22
RELAY_LAG = 5
DIRECT = (2, 1, 4)
DIRECT_WRAP = 3
WRAP_START = 4
WRAP_STEPS = 2
SPAN = 8


def flip(index):
    return index + 1 - 2 * lax.rem(index, 2)


def clip(value, low, high):
    return jnp.minimum(jnp.maximum(value, low), high)


def step_kernel(
    n_walk, n_vec, owners, chol, walkers, table, partner, beyond,
    home, away, up, down, mat, hold, state, acc, result, note, told,
    home_sem, away_sem, up_sem, down_sem,
    mate_send, across_send, relay_send, up_send, down_send,
    x_send, y_send, d_send, r_send, zy_send, zd_send, zr_send, z_send, direct_send, hold_send, hold_sem,
    x_sem, y_sem, z_sem, zy_sem, d_sem, r_sem, zd_sem, zr_sem,
    load_sem, keep_sem, note_send, note_sem, t_send, t_sem,
):
    walk, vec = lax.axis_index("walk"), lax.axis_index("vec")
    rows = n_walk // 2
    last = rows - 1
    row, col = walk // 2, lax.rem(walk, 2)
    low = lax.rem(vec, 2)
    hub = low == col
    leaf = jnp.logical_not(hub)
    pieces, electrons = home.shape[0], home.shape[1]
    blocks = pieces // DEEP
    per_dev = walkers.shape[0]
    quarter = walkers.shape[1] // n_vec
    units = quarter // UNIT
    groups = [(first, min(GROUP, units - first)) for first in range(0, units, GROUP)]
    ends = [first + size for first, size in groups]
    flip_walk, flip_vec = flip(walk), flip(vec)
    far_vec = lax.rem(vec + 2, n_vec)
    z_next = lax.rem(row + 1 - 2 * col + rows, rows)
    order = jnp.where(col == 0, row, last - row)
    order_own = last - order
    z_own = lax.rem(row + 2 * col - 1 + rows, rows)
    direct_to = {"walk": z_own * 2 + col, "vec": vec}
    z_to = {"walk": z_next * 2 + col, "vec": vec}
    across = {"walk": flip_walk, "vec": vec}
    mate = {"walk": walk, "vec": flip_vec}
    over = {"walk": walk, "vec": far_vec}
    above = {"walk": walk + 2, "vec": vec}
    below = {"walk": walk - 2, "vec": vec}
    row_up, row_down = lax.rem(row + 1, rows), lax.rem(row + rows - 1, rows)

    place = col * n_vec + vec
    readers = [({"walk": walk, "vec": lax.rem(vec + j, n_vec)}, place) for j in range(1, n_vec)]
    readers += [({"walk": flip_walk, "vec": lax.rem(vec + j, n_vec)}, place) for j in range(n_vec)]
    readers += [({"walk": row_up * 2, "vec": lax.rem(vec + j, n_vec)}, place + 2 * n_vec) for j in range(n_vec)]
    readers += [({"walk": row_down * 2 + 1, "vec": lax.rem(vec + j, n_vec)}, place + 2 * n_vec) for j in range(n_vec)]

    def each(lo, hi, f):
        def body(k, carry):
            f(k)
            return carry
        lax.fori_loop(lo, hi, body, 0)

    def remote(src, dst, send, recv, target):
        return pltpu.make_async_remote_copy(
            src_ref=src, dst_ref=dst, send_sem=send, recv_sem=recv,
            device_id=target, device_id_type=MESH)

    def chol_piece(k):
        b, j = lax.div(k, DEEP), lax.rem(k, DEEP)
        half = DEEP // 2
        at = b * half + jnp.where(j < half, j, j - half + blocks * half)
        return chol.at[0, 0, :, pl.ds(pl.multiple_of(at * LANES, LANES), LANES)]

    def own_to_home(k):
        return pltpu.make_async_copy(chol_piece(k), home.at[k], home_sem.at[lax.div(k, BATCH)])

    def home_batch(k):
        return home.at[pl.ds(k, BATCH)]

    def own_to_mate(k):
        return remote(chol_piece(k), home.at[k], mate_send, home_sem.at[lax.div(k, BATCH)], mate)

    def own_across(k):
        return remote(chol_piece(k), away.at[k], across_send, away_sem.at[k], across)

    def away_to_mate(k):
        return remote(away.at[k], away.at[k], relay_send, away_sem.at[k], mate)

    def send_up(k):
        return remote(up.at[k], up.at[k], up_send, up_sem.at[lax.rem(k, up_sem.shape[0])], above)

    def send_down(k):
        return remote(down.at[k], down.at[k], down_send, down_sem.at[lax.rem(k, down_sem.shape[0])], below)

    def unit_rows(u):
        return pl.ds(pl.multiple_of(vec * quarter + u * UNIT, UNIT), UNIT)

    def x_unit(u):
        at = unit_rows(u)
        return remote(walkers.at[:, at], partner.at[:, at], x_send, x_sem.at[lax.div(u, GROUP)], across)

    def z_unit(u):
        at = unit_rows(u)
        return remote(partner.at[:, at], beyond.at[:, at], z_send, z_sem.at[lax.div(u, GROUP)], z_to)

    def direct_unit(u):
        at = unit_rows(u)
        return remote(walkers.at[:, at], hold.at[u], direct_send.at[u], hold_sem.at[u], direct_to)

    def relay_unit(u):
        at = unit_rows(u)
        return remote(hold.at[u], beyond.at[:, at], hold_send.at[u], z_sem.at[lax.div(u, GROUP)], across)

    def direct_count(position):
        return jnp.where(position == last, DIRECT_WRAP,
                         jnp.minimum(DIRECT[0] + DIRECT[1] * position, DIRECT[2]))

    def relay_all():
        def one(u):
            direct_unit(u).wait_recv()
            relay_unit(u).start()
        each(0, direct_count(lax.rem(order_own + last, rows)), one)

    def direct_sent(i):
        paced = clip(lax.div(i - WRAP_START + WRAP_STEPS, WRAP_STEPS), 0, DIRECT_WRAP)
        return jnp.where(order_own == last, paced, direct_count(order_own))

    def group(buffer, n, index, send, recv, target):
        first, size = groups[n]
        at = pl.ds(pl.multiple_of(index * quarter + first * UNIT, UNIT), size * UNIT)
        return remote(buffer.at[:, at], buffer.at[:, at], send, recv, target)

    def quarter_of(buffer, send, recv):
        at = pl.ds(pl.multiple_of(vec * quarter, UNIT), quarter)
        return remote(buffer.at[:, at], buffer.at[:, at], send, recv, mate)

    def load(w):
        src = walkers.at[w] if w < per_dev else partner.at[w - per_dev]
        return pltpu.make_async_copy(src, state.at[w], load_sem.at[w])

    bar = pltpu.get_barrier_semaphore()
    for target in (
        [t for t, _ in readers[:2 * n_vec - 1]]
        + [{"walk": r * 2 + c, "vec": lax.rem(vec + j, n_vec)}
           for r in (row_up, row_down) for c in range(2) for j in range(n_vec)]
    ):
        pl.semaphore_signal(bar, inc=1, device_id=target, device_id_type=MESH)
    for w in range(per_dev):
        load(w).start()

    @pl.when(hub)
    def _():
        each(0, pieces, lambda k: own_to_home(k).start())

    def code_of(root):
        here = (lax.div(root, 2) == row).astype(jnp.float32)
        under = (lax.div(root, 2) <= row).astype(jnp.float32)
        at_home = (lax.rem(root, 2) == col).astype(jnp.float32)
        return here + 2.0 * under + 4.0 * at_home

    code_mate = jnp.where(low == 0, code_of(owners[0, 1]), code_of(owners[0, 0]))
    code_own = jnp.where(low == 0, code_of(owners[0, 0]), code_of(owners[0, 1]))
    note[...] = jnp.full(note.shape, code_mate, jnp.float32)

    @pl.when(hub)
    def _():
        told[...] = jnp.full(told.shape, code_own, jnp.float32)

    send_note = remote(note, told, note_send, note_sem, mate)

    pl.semaphore_wait(bar, 6 * n_vec - 1)

    each(0, direct_sent(0), lambda u: direct_unit(u).start())

    @pl.when(hub)
    def _():
        send_note.start()
        each(0, min(AHEAD, pieces), lambda k: own_to_mate(k).start())

    @pl.when(leaf)
    def _():
        def x_count(k):
            slow = lax.div(jnp.minimum(k, X_SLOW[0]), X_SLOW[1])
            return jnp.minimum(slow + jnp.maximum(k - X_SLOW[0], 0) * X_FAST, units)

        def start(k):
            own_across(k).start()
            each(x_count(k), x_count(k + 1), lambda u: x_unit(u).start())
        each(0, pieces, start)
        each(x_count(pieces), units, lambda u: x_unit(u).start())

    acc[...] = jnp.zeros_like(acc)

    @pl.when(leaf)
    def _():
        send_note.wait_recv()

    code = jnp.max(told[...])
    from_home = code >= 4.0
    code = jnp.where(from_home, code - 4.0, code)
    below_or_here = code >= 2.0
    here = jnp.where(below_or_here, code - 2.0, code) >= 1.0
    total = pieces + SKEW * last
    depth = jnp.maximum(row, last - row)

    skip = direct_count(order)

    def sent(i):
        gone = jnp.where(
            hub,
            lax.div(jnp.maximum(i - Z_HUB[0], 0) * (units - skip), Z_HUB[1] - Z_HUB[0]),
            lax.div(jnp.maximum(i - Z_LEAF[0], 0) * (units - skip), Z_LEAF[1] - Z_LEAF[0]))
        return jnp.minimum(skip + gone, units)

    def chain(i):
        @pl.when(i < pieces)
        def _():
            @pl.when(hub)
            def _():
                own_across(i).wait_recv()
                away_to_mate(i).start()

                @pl.when(i + AHEAD < pieces)
                def _():
                    own_to_mate(i + AHEAD).start()

                @pl.when(lax.rem(i, BATCH) == 0)
                def _():
                    pltpu.make_async_copy(home_batch(i), home_batch(i), home_sem.at[lax.div(i, BATCH)]).wait()

            @pl.when(leaf)
            def _():
                @pl.when(lax.rem(i, BATCH) == 0)
                def _():
                    remote(home_batch(i), home_batch(i), mate_send, home_sem.at[lax.div(i, BATCH)], mate).wait_recv()

                away_to_mate(i).wait_recv()

        ku = i - SKEW * row
        kd = i - SKEW * (last - row)

        @pl.when(jnp.logical_and(ku >= 0, ku < pieces))
        def _():
            own = jnp.where(from_home, home[ku], away[ku])

            @pl.when(row == 0)
            def _():
                up[ku] = own

            @pl.when(row > 0)
            def _():
                send_up(ku).wait_recv()
                up[ku] = jnp.where(here, own, up[ku])

            @pl.when(row < last)
            def _():
                send_up(ku).start()

        @pl.when(jnp.logical_and(kd >= 0, kd < pieces))
        def _():
            own = jnp.where(from_home, home[kd], away[kd])

            @pl.when(row == last)
            def _():
                down[kd] = own

            @pl.when(row < last)
            def _():
                send_down(kd).wait_recv()
                down[kd] = jnp.where(here, own, down[kd])

            @pl.when(row > 0)
            def _():
                send_down(kd).start()

        done = i - SKEW * depth

        @pl.when(jnp.logical_and(done >= 0, done < pieces))
        def _():
            mat[done] = jnp.where(below_or_here, up[done], down[done])

    load_at = X_HUB[-1] + Y_LAG + LOAD_LAG

    def arrive(n):
        group(partner, n, vec, x_send, x_sem.at[n], across).wait_recv()
        group(partner, n, vec, y_send, y_sem.at[n], over).start()
        group(partner, n, vec, d_send, d_sem, mate).start()

    def pass_on(n):
        group(partner, n, far_vec, y_send, y_sem.at[n], over).wait_recv()
        group(partner, n, far_vec, r_send, r_sem, mate).start()

    def load_partner():
        quarter_of(partner, d_send, d_sem).wait_recv()
        quarter_of(partner, r_send, r_sem).wait_recv()
        for w in range(per_dev):
            load(per_dev + w).start()

    def loaded(first):
        for w in range(per_dev):
            load(first + w).wait()

    def z_arrive(n):
        group(beyond, n, vec, zy_send, z_sem.at[n], z_to).wait_recv()
        group(beyond, n, vec, zy_send, zy_sem.at[n], over).start()
        group(beyond, n, vec, zd_send, zd_sem, mate).start()

    def z_pass_on(n):
        group(beyond, n, far_vec, zy_send, zy_sem.at[n], over).wait_recv()
        group(beyond, n, far_vec, zr_send, zr_sem, mate).start()

    half = DEEP // 2
    wide = half * LANES

    def multiply(b, w):
        p = state[w, pl.ds(pl.multiple_of(b * wide, wide), wide), :]
        re = jnp.concatenate([mat[b * DEEP + j] for j in range(half)], axis=1)
        im = jnp.concatenate([mat[b * DEEP + half + j] for j in range(half)], axis=1)
        x = jnp.dot(re, p, preferred_element_type=jnp.float32)
        y = jnp.dot(im, p, preferred_element_type=jnp.float32)
        acc[w, :, :electrons] += x[:, :electrons] - y[:, electrons:]
        acc[w, :, electrons:] += x[:, electrons:] + y[:, :electrons]

    def products(i):
        e = i - SKEW * depth - (DEEP - 1)
        def own_count(e, w):
            return clip(lax.div(e + DEEP - w, DEEP), 0, blocks)

        def partner_count(i, w):
            e = i - SKEW * depth - (DEEP - 1)
            full = clip(lax.div(e + DEEP, DEEP), 0, blocks)
            return jnp.where(i > total, blocks, clip((i - load_at - 2) * CATCH_UP, 0, full))

        spans = [(own_count(e - 1, w), own_count(e, w)) for w in range(per_dev)]
        spans += [(partner_count(i - 1, w), partner_count(i, w)) for w in range(per_dev)]
        def some(w, carry):
            lo, hi = spans[-1]
            for v in range(len(spans) - 1):
                lo = jnp.where(w == v, spans[v][0], lo)
                hi = jnp.where(w == v, spans[v][1], hi)
            lax.fori_loop(lo, hi, lambda b, c: (multiply(b, w), c)[1], 0)
            return carry
        lax.fori_loop(0, len(spans), some, 0)

    sub = lax.broadcasted_iota(jnp.int32, result.shape, 0)
    lane = lax.broadcasted_iota(jnp.int32, result.shape, 1)
    result[...] = jnp.zeros_like(result)
    orbitals = blocks * wide

    def finish(w):
        o = state[w, orbitals:, :]
        m = acc[w].astype(jnp.bfloat16)
        u = jnp.dot(m[:, :electrons], o, preferred_element_type=jnp.float32)
        v = jnp.dot(m[:, electrons:], o, preferred_element_type=jnp.float32)
        g_re = u[:, :electrons] - v[:, electrons:]
        g_im = u[:, electrons:] + v[:, :electrons]
        side = LANES if electrons % LANES == 0 else electrons
        eye = (lax.broadcasted_iota(jnp.int32, (side, side), 0)
               == lax.broadcasted_iota(jnp.int32, (side, side), 1))
        spots = range(0, electrons, side)

        def tile(g, a, b):
            return g[a:a + side, b:b + side]

        ex_re = ex_im = bias_re = bias_im = jnp.zeros((side, side), jnp.float32)
        for a in spots:
            bias_re = bias_re + tile(g_re, a, a)
            bias_im = bias_im + tile(g_im, a, a)
            for b in spots:
                if b < a:
                    continue
                times = 1.0 if a == b else 2.0
                re, im = tile(g_re, a, b), tile(g_im, a, b)
                t_re, t_im = tile(g_re, b, a).T, tile(g_im, b, a).T
                ex_re = ex_re + times * (re * t_re - im * t_im)
                ex_im = ex_im + times * (re * t_im + im * t_re)
        values = [
            jnp.sum(jnp.where(eye, bias_re, 0.0)),
            jnp.sum(jnp.where(eye, bias_im, 0.0)),
            jnp.sum(ex_re),
            jnp.sum(ex_im),
        ]
        for n, value in enumerate(values):
            result[...] = jnp.where(jnp.logical_and(sub == w, lane == n), value, result[...])

    def tell(n):
        target, where = readers[n]
        return remote(result, table.at[where], t_send, t_sem, target)

    keep = pltpu.make_async_copy(result, table.at[place], keep_sem)

    def tell_all():
        for n in range(len(readers)):
            tell(n).start()
        keep.start()

    def hub_units():
        each(0, units, lambda u: x_unit(u).start())

    events, rest = [], []
    events.append((HUB_START, hub, functools.partial(hub_units)))
    for times, z_times, role in ((X_HUB, Z_HUB, hub), (X_LEAF, Z_LEAF, leaf)):
        late = []
        for n, end in enumerate(ends):
            at = times[min(n, len(times) - 1)]
            events.append((at, role, functools.partial(arrive, n)))
            events.append((at + Y_LAG, role, functools.partial(pass_on, n)))
            fewest = min(DIRECT[0], DIRECT_WRAP)
            span = z_times[1] - z_times[0]
            at = z_times[0] + -(-max(end - fewest, 0) * span // (units - fewest)) + Z_LAG
            if groups[n][0] < max(DIRECT[2], DIRECT_WRAP):
                at = max(at, RELAY + RELAY_LAG)
            for run, when in ((z_arrive, at), (z_pass_on, at + Z_LAG_Y)):
                if when < min(total, NEAR):
                    events.append((when, role, functools.partial(run, n)))
                else:
                    late.append((run, n))
        late.sort(key=lambda item: item[1] + (1 if item[0] is z_pass_on else 0))
        rest.append((role, late))
    events.append((RELAY, None, functools.partial(relay_all)))
    events.append((load_at, None, functools.partial(load_partner)))
    events.append((load_at + 2, None, functools.partial(loaded, per_dev)))
    events.append((min(DEEP - 1 + SKEW * (rows // 2), total), None, functools.partial(loaded, 0)))

    def handle(start, stop):
        for role, late in rest:
            @pl.when(role)
            def _():
                for run, n in late[start:stop]:
                    run(n)

    after = [
        lambda: each(sent(total - 1), units, lambda u: z_unit(u).start()),
        functools.partial(handle, 0, 1),
        lambda: each(total, total + 2, products),
    ]
    for w in range(2 * per_dev):
        after.append(functools.partial(handle, w + 1, w + 2))
        after.append(functools.partial(finish, w))
    after.append(tell_all)
    after.append(functools.partial(handle, 2 * per_dev + 1, 10 * len(groups)))

    families = {}
    for when, role, run in events:
        families.setdefault((run.func, when // SPAN) if role is not None else None, []).append((when, role, run))

    def step(i):
        chain(i)
        for members in families.values():
            times = [when for when, _, _ in members]

            @pl.when(jnp.logical_and(i >= min(times), i <= max(times)))
            def _():
                for when, role, run in members:
                    pl.when(i == when if role is None else jnp.logical_and(i == when, role))(run)
        each(jnp.where(i == 0, direct_sent(0), direct_sent(i - 1)), direct_sent(i), lambda u: direct_unit(u).start())
        each(sent(i - 1), sent(i), lambda u: z_unit(u).start())
        products(i)

    each(0, total, step)
    for run in after:
        run()


    quarter_of(beyond, zd_send, zd_sem).wait_recv()
    quarter_of(beyond, zr_send, zr_sem).wait_recv()

    def all_sent(buffer, send, target):
        remote(buffer, buffer, send, t_sem, target).wait_send()

    @pl.when(hub)
    def _():
        send_note.wait_send()
        all_sent(home, mate_send, mate)
        all_sent(away, relay_send, mate)

    @pl.when(leaf)
    def _():
        all_sent(away, across_send, across)

    @pl.when(row < last)
    def _():
        all_sent(up, up_send, above)

    @pl.when(row > 0)
    def _():
        all_sent(down, down_send, below)

    part = partner.at[:, pl.ds(pl.multiple_of(vec * quarter, UNIT), quarter)]
    for send, target in (
        (x_send, across), (y_send, over), (d_send, mate), (r_send, mate),
        (zy_send, over), (zd_send, mate), (zr_send, mate),
    ):
        all_sent(part, send, target)

    keep.wait()
    for count in range(min(DIRECT[0], DIRECT_WRAP), max(DIRECT[2], DIRECT_WRAP) + 1):
        @pl.when(skip == count)
        def _():
            some = partner.at[:, pl.ds(0, (units - count) * UNIT)]
            all_sent(some, z_send, z_to)

    each(0, direct_count(order_own), lambda u: direct_unit(u).wait_send())
    each(0, direct_count(lax.rem(order_own + last, rows)), lambda u: relay_unit(u).wait_send())

    heard = table.at[pl.ds(0, len(readers))]
    remote(heard, heard, t_send, t_sem, mate).wait_send()

    remote(heard, heard, t_send, t_sem, mate).wait_recv()


def step_all(n_walk, n_vec, owners, chol, walkers):
    per_dev, height, width = walkers.shape
    electrons, orbitals = chol.shape[2:]
    pieces = orbitals // LANES
    units = height // n_vec // UNIT
    groups = -(-units // GROUP)
    most = max(DIRECT[2], DIRECT_WRAP)
    ring = RING if SKEW * (n_walk // 2 - 1) < RING < pieces else pieces
    big = pltpu.VMEM((pieces, electrons, LANES), chol.dtype)
    dma = pltpu.SemaphoreType.DMA
    any_spec = pl.BlockSpec(memory_space=pl.ANY)
    smem = pl.BlockSpec(memory_space=pltpu.SMEM)
    same = jax.ShapeDtypeStruct(walkers.shape, walkers.dtype)
    return pl.pallas_call(
        functools.partial(step_kernel, n_walk, n_vec),
        out_shape=(jax.ShapeDtypeStruct((4 * n_vec, 8, 128), jnp.float32), same, same),
        in_specs=[smem, any_spec, any_spec],
        out_specs=(any_spec, any_spec, any_spec),
        scratch_shapes=[
            big, big, big, big, big,
            pltpu.VMEM((max(DIRECT[2], DIRECT_WRAP), per_dev, UNIT, width), walkers.dtype),
            pltpu.VMEM((2 * per_dev, height, width), walkers.dtype),
            pltpu.VMEM((2 * per_dev, electrons, width), jnp.float32),
            pltpu.VMEM((8, 128), jnp.float32),
            pltpu.VMEM((8, 128), jnp.float32),
            pltpu.VMEM((8, 128), jnp.float32),
        ] + [dma((-(-pieces // BATCH),))] + [dma((pieces,))] + [dma((ring,))] * 2 + [dma] * 12 + [dma] + [dma((most,))] * 3 + [dma((groups,))] * 4 + [dma] * 4
        + [dma((2 * per_dev,)), dma, dma, dma, dma, dma],
        compiler_params=pltpu.CompilerParams(
            collective_id=0, has_side_effects=True, vmem_limit_bytes=62 * 1024 * 1024),
        name="step_all",
    )(owners, chol, walkers)


BITS = 4


def branch_kernel(
    n_walk, n_vec, slots, walkers, partner, beyond, table,
    branched, bias, energy, held, facts, in_sem, out_sem, t_sem,
):
    walk, vec = lax.axis_index("walk"), lax.axis_index("vec")
    col = lax.rem(walk, 2)
    per_dev, height = walkers.shape[:2]
    piece = height // BITS
    total = per_dev * n_walk

    def rows(t):
        return pl.ds(t * piece, piece)

    def fetch(buffer, w, s, t):
        return pltpu.make_async_copy(buffer.at[w, rows(t)], held.at[s, rows(t)], in_sem.at[s, t])

    def put(s, t):
        return pltpu.make_async_copy(held.at[s, rows(t)], branched.at[s, rows(t)], out_sem.at[s, t])

    cases = [(s, t) for s in range(per_dev) for t in range(BITS)]
    picks = []
    for s in range(per_dev):
        relative = lax.rem(slots[s] - (walk - 1) * per_dev + total, total)
        side, w = lax.div(relative, per_dev), lax.rem(relative, per_dev)
        mine, beside = side == 1, side == 2 * (1 - col)
        far = jnp.logical_not(jnp.logical_or(mine, beside))
        picks.append((w, jnp.where(far, 1, 0), jnp.where(mine, col, 1 - col)))
        for wanted, buffer in ((mine, walkers), (beside, partner), (far, beyond)):
            @pl.when(wanted)
            def _():
                for t in range(BITS):
                    fetch(buffer, w, s, t).start()
    facts_in = pltpu.make_async_copy(table, facts, t_sem)
    facts_in.start()
    for s, t in cases:
        fetch(walkers, 0, s, t).wait()
        put(s, t).start()
    facts_in.wait()

    for s, (w, far, block) in enumerate(picks):
        def value(v, g, lane):
            sender = lax.rem(v, 2)
            at = far * 2 * n_vec + sender * n_vec + lax.div(v, 2) * 2 + g
            return facts[at, jnp.where(block == sender, 0, per_dev) + w, lane]

        for g in range(2):
            for part in range(2):
                bias[s, g, part] = value(vec, g, part)
        for part in range(2):
            energy[s, part] = -0.5 * sum(value(jnp.int32(v), g, 2 + part) for v in range(n_vec) for g in range(2))

    for s, t in cases:
        put(s, t).wait()


def branch(n_walk, n_vec, slots, walkers, partner, beyond, table):
    per_dev = walkers.shape[0]
    dma = pltpu.SemaphoreType.DMA
    any_spec = pl.BlockSpec(memory_space=pl.ANY)
    smem = pl.BlockSpec(memory_space=pltpu.SMEM)
    return pl.pallas_call(
        functools.partial(branch_kernel, n_walk, n_vec),
        out_shape=(
            jax.ShapeDtypeStruct(walkers.shape, walkers.dtype),
            jax.ShapeDtypeStruct((per_dev, 2, 2), jnp.float32),
            jax.ShapeDtypeStruct((per_dev, 2), jnp.float32),
        ),
        in_specs=[smem, any_spec, any_spec, any_spec, any_spec],
        out_specs=(any_spec, smem, smem),
        scratch_shapes=[
            pltpu.VMEM(walkers.shape, walkers.dtype), pltpu.SMEM(table.shape, table.dtype),
            dma((per_dev, BITS)), dma((per_dev, BITS)), dma,
        ],
        compiler_params=pltpu.CompilerParams(vmem_limit_bytes=62 * 1024 * 1024),
        name="branch",
    )(slots, walkers, partner, beyond, table)


def shards(n_walk, n_vec, walkers, chol, owners, branch_src):
    table, partner, beyond = step_all(n_walk, n_vec, owners, chol, walkers)
    return branch(n_walk, n_vec, branch_src, walkers, partner, beyond, table)


def solution(mesh):
    n_walk, n_vec = mesh.shape["walk"], mesh.shape["vec"]
    return jax.shard_map(
        functools.partial(shards, n_walk, n_vec),
        mesh=mesh,
        in_specs=(P("walk", None, None), P("vec", "walk", None, None), P("vec", None), P("walk")),
        out_specs=(P("walk", None, None), P("walk", "vec", None), P("walk", None)),
        check_vma=False,
    )
```
